768 devices in a mesh: rep: 96 (over z, y), fsdp: 8 (over x, core).
Axes of the slice: x: 4, y: 8, z: 12, core: 2. Of those that a mesh axis runs over, the one named last changes fastest.
Arguments:
- deltas: bfloat16 [96, 48, 8192], P('rep', 'fsdp'), may hold values from -24 to 24, as said below
- momentum: float32 [48, 8192], P('fsdp'), may hold values from -6 to 6
- master: float32 [48, 8192], P('fsdp'), may hold values from -6 to 6
Outputs:
- new_momentum: float32 [48, 8192], P('fsdp')
- new_master: float32 [48, 8192], P('fsdp')
- full_weights: bfloat16 [48, 8192], replicated
The draws below stay inside these ranges and needn't reach their ends.
Inputs may be any that keep to these rules, and one draw needn't show every extreme that they name: `deltas`: each replica's pseudo-gradient entries.
All inputs are finite; a program needn't handle non-finite values.
Results may differ from the reference program's by a relative error of at most 0.0004.
Values may be sent and summed in bfloat16 or wider, within the bound.
A program may use at most 32 MiB of HBM per device.

```python
import jax
import jax.numpy as jnp
from jax import lax

D = 8192
ITERS = 3
REPS = 96
ROWS = 48


def draw_deltas(key, part=0):
    key_scale = jax.random.fold_in(key, 0)
    key_common = jax.random.fold_in(key, 1)
    key_noise = jax.random.fold_in(key, 2)
    key_bias = jax.random.fold_in(key, 4)
    key_pick = jax.random.fold_in(key, 5)
    ramp = jnp.arange(REPS, dtype=jnp.float32) / max(REPS - 1, 1)
    scales = 0.1 * 10.0 ** ramp * jax.random.uniform(key_scale, (REPS,), jnp.float32, 0.8, 1.25)
    order = jax.random.permutation(key_pick, REPS)
    outlier = (order < 3 * REPS // 8).astype(jnp.float32)
    scales = outlier * 0.5 + (1.0 - outlier) * scales
    row_pos = jnp.arange(ROWS, dtype=jnp.float32) / max(ROWS - 1, 1)
    bias_rows = 0.7 * 3.0 ** row_pos
    bias = 2.2 * bias_rows[:, None] * jax.random.normal(key_bias, (ROWS, D), jnp.float32)
    common = 0.5 * jax.random.normal(key_common, (ROWS, D), jnp.float32)
    noise = jax.random.normal(key_noise, (REPS, ROWS, D), jnp.float32)
    values = common[None] + outlier[:, None, None] * bias[None] + scales[:, None, None] * noise
    return jnp.clip(values, -24.0, 24.0).astype(jnp.bfloat16)


def level_of(key, dims, shards, low, top_value):
    level, own = 1.0, jax.random.fold_in(key, 6)
    for axis_at, shards_of in shards:
        heights = jnp.exp(jax.random.uniform(jax.random.fold_in(own, axis_at), (shards_of,), jnp.float32, low / len(shards), top_value / len(shards)))
        level = level * jnp.repeat(heights, dims[axis_at] // shards_of).reshape([-1 if axis == axis_at else 1 for axis in range(len(dims))])
    return level


def normal_values(own_key, dims, scale, limit, pieces=(), kind=jnp.bfloat16):
    result = jax.random.normal(own_key, dims, jnp.float32) * scale
    if len(pieces) > 0:
        result = level_of(own_key, dims, pieces, -0.22, 0.18) * result
    return jnp.clip(result, min=-limit, max=limit).astype(kind)


def setup_inputs(seed: int = 0) -> dict:
    key_list = jax.random.split(jax.random.key(seed), 4)
    return {
        "deltas": draw_deltas(jax.random.fold_in(key_list[3], 71), 0),
        "momentum": normal_values(key_list[1], (ROWS, D), 0.5, 6.0, ((0, 8),), jnp.float32),
        "master": normal_values(key_list[2], (ROWS, D), 1.0, 6.0, ((0, 8),), jnp.float32),
    }


EPS = 1e-06

def reference(deltas, momentum, master):
    values = deltas.astype(jnp.float32)
    center = jnp.zeros((ROWS, D), jnp.float32)
    for step in range(ITERS):
        spread = values - center[None]
        dist2 = lax.optimization_barrier(jnp.sum(spread * spread, axis=(1, 2)))
        weight = 1.0 / jnp.sqrt(dist2 / (ROWS * D) + EPS)
        numer = lax.optimization_barrier(jnp.sum(weight[:, None, None] * values, axis=0))
        center = numer / jnp.sum(weight)
    new_momentum = 0.9 * momentum + center
    new_master = master - 0.7 * (center + 0.9 * new_momentum)
    return (new_momentum, new_master, new_master.astype(jnp.bfloat16))
```

```python
import functools

import jax
import jax.numpy as jnp
from jax import lax
from jax.experimental import pallas as pl
from jax.experimental.pallas import tpu as pltpu
from jax.sharding import PartitionSpec as P

ITERS = 3
EPS = 1e-06
NY = 8
LANES = 128
MESH = pl.DeviceIdType.MESH
F32, BF16 = jnp.float32, jnp.bfloat16


def split3(value):
    high = value.astype(BF16)
    rest = value - high.astype(F32)
    mid = rest.astype(BF16)
    low = (rest - mid.astype(F32)).astype(BF16)
    return high, mid, low


def kernel(
    nf, nz, delta, mom, mas, nm, ns, fw,
    own, ra, rf, tb, zb, zq, xs, ys, zs, cd, cn, nd, wb, wf,
    local_sem, a_sem, b_sem, x_sem, y_sem, z_sem, cz_sem, cy_send, cy_recv, w_send, w_recv,
):
    rows, width = own.shape
    block = width // NY
    halves = nz // rows
    chunk = block // halves
    tiles = block // LANES
    parts = chunk // LANES
    reps = NY * nz
    entries = nf * rows * width

    rep, f = lax.axis_index("rep"), lax.axis_index("fsdp")
    y, z = lax.rem(rep, NY), lax.div(rep, NY)

    def peers(axis, n, me, visit):
        def step(i, carry):
            half = lax.div(i + 1, 2)
            place = lax.rem(me + n // 2 + half * (2 * lax.rem(i, 2) - 1) + n, n)
            if axis == "x":
                device = (rep, place)
            elif axis == "y":
                device = (z * NY + place, f)
            else:
                device = (place * NY + y, f)
            visit(device, place)
            return carry

        lax.fori_loop(0, n - 1, step, 0)

    def send(src, dst, send_sem, recv_sem, device):
        pltpu.make_async_remote_copy(
            src_ref=src, dst_ref=dst, send_sem=send_sem, recv_sem=recv_sem,
            device_id=device, device_id_type=MESH,
        ).start()

    def drain(ref, sem):
        pltpu.make_async_copy(ref, ref, sem).wait()

    own_copy = pltpu.make_async_copy(delta.at[0], own, local_sem.at[0])
    own_copy.start()
    mine = pl.ds(pl.multiple_of(y * block, block), block)
    block_copy = pltpu.make_async_copy(delta.at[0, :, mine], ra.at[y], local_sem.at[1])
    block_copy.start()

    barrier = pltpu.get_barrier_semaphore()

    def greet(device, place):
        pl.semaphore_signal(barrier, inc=1, device_id=device, device_id_type=MESH)

    peers("x", nf, f, greet)
    peers("y", NY, y, greet)
    peers("z", nz, z, greet)
    pl.semaphore_wait(barrier, nf + NY + nz - 3)

    def send_a(device, place):
        columns = pl.ds(pl.multiple_of(place * block, block), block)
        send(delta.at[0, :, columns], ra.at[y], a_sem.at[0], a_sem.at[1], device)

    peers("y", NY, y, send_a)

    def exchange(axis, n, me, buffer, sems, row):
        buffer[me] = row
        peers(axis, n, me, lambda device, place: send(buffer.at[me], buffer.at[me], sems.at[0], sems.at[1], device))
        drain(buffer.at[pl.ds(0, n - 1)], sems.at[1])
        return jnp.sum(buffer[...], axis=0)

    def x_stage(k, row):
        return exchange("x", nf, f, xs.at[k], x_sem.at[k], row)

    def y_stage(k, row):
        return exchange("y", NY, y, ys.at[k], y_sem.at[k], row)

    def z_stage(k, row):
        return exchange("z", nz, z, zs.at[k], z_sem.at[k], row)

    lane = lax.broadcasted_iota(jnp.int32, (1, LANES), 1)

    own_copy.wait()
    value = own[...].astype(F32)
    squared = jnp.sum(jnp.sum(value * value, axis=0, keepdims=True), axis=1, keepdims=True)
    row = jnp.where(lane == rep, squared, 0.0)
    row = y_stage(0, x_stage(0, row))

    block_copy.wait()
    drain(ra.at[pl.ds(0, NY - 1)], a_sem.at[1])
    for k in range(NY):
        arrived = ra[k].astype(F32)
        for j in range(tiles):
            rf[pl.ds(8 * (j * NY + k), rows), :] = arrived[:, j * LANES : (j + 1) * LANES]
    for r in range(rows):
        for j in range(tiles):
            column = pl.ds(j * LANES, LANES)
            tb[r, :, column] = rf[pl.ds(8 * j * NY + r, NY, stride=8), :].astype(BF16)

    def piece(place):
        columns = pl.ds(pl.multiple_of(lax.rem(place, halves) * chunk, chunk), chunk)
        return tb.at[lax.div(place, halves), :, columns]

    peers("z", nz, z, lambda device, place: send(piece(place), zb.at[z], b_sem.at[0], b_sem.at[1], device))
    zb[z] = piece(z)[...]
    zq[pl.ds(reps, LANES - reps), :] = jnp.zeros((LANES - reps, LANES), F32)

    row = z_stage(0, row)
    drain(zb.at[pl.ds(0, nz - 1)], b_sem.at[1])
    held = zb[...].reshape(reps, chunk)

    def center_of(squared):
        weight = jnp.where(lane < reps, 1.0 / jnp.sqrt(squared / entries + EPS), 0.0)
        share = weight / jnp.sum(weight, axis=1, keepdims=True)
        left = jnp.concatenate(split3(share), axis=0)[:, :reps]
        return jnp.sum(jnp.dot(left, held, preferred_element_type=F32), axis=0, keepdims=True)

    center = center_of(row)
    for k in range(1, ITERS):
        spread = held.astype(F32) - center
        spread = spread * spread
        total = spread[:, :LANES]
        for part in range(1, parts):
            total = total + spread[:, part * LANES : (part + 1) * LANES]
        zq[pl.ds(0, reps), :] = total
        row = lax.dot_general(
            jnp.ones((8, LANES), F32), zq[...], (((1,), (1,)), ((), ())),
            precision=lax.Precision.HIGHEST, preferred_element_type=F32,
        )[:1]
        center = center_of(z_stage(k, y_stage(k, x_stage(k, row))))

    for part in range(parts):
        cd[y, z, pl.ds(part, 1), :] = center[:, part * LANES : (part + 1) * LANES]
    peers("z", nz, z, lambda device, place: send(cd.at[y, z], cd.at[y, z], cz_sem.at[0], cz_sem.at[1], device))
    drain(cd.at[0, pl.ds(0, nz - 1)], cz_sem.at[1])
    peers("y", NY, y, lambda device, place: send(cd.at[y], cd.at[y], cy_send.at[0], cy_recv.at[y], device))

    def update(i, carry):
        half = lax.div(i, 2) + lax.rem(i, 2)
        b = lax.rem(y + half * (1 - 2 * lax.rem(i, 2)) + NY, NY)

        @pl.when(i > 0)
        def _():
            drain(cd.at[b], cy_recv.at[b])

        for k in range(nz):
            cn[pl.ds(k * parts, parts), :] = cd[b, k]
        for j in range(tiles):
            here = pl.ds(pl.multiple_of(b * block + j * LANES, LANES), LANES)
            there = pl.ds(j, rows, stride=tiles)
            c = cn[there, :]
            momentum = 0.9 * mom[:, here] + c
            master = mas[:, here] - 0.7 * (c + 0.9 * momentum)
            nm[:, here] = momentum
            ns[:, here] = master
            nd[there, :] = master
        wb[f, b] = nd[...].astype(BF16)
        peers("x", nf, f, lambda device, place: send(wb.at[f, b], wb.at[f, b], w_send.at[0], w_recv.at[b], device))
        return carry

    lax.fori_loop(0, NY, update, 0)

    def place_weights(i, carry):
        half = lax.div(i, 2) + lax.rem(i, 2)
        b = lax.rem(y + half * (1 - 2 * lax.rem(i, 2)) + NY, NY)
        drain(wb.at[pl.ds(0, nf - 1), b], w_recv.at[b])
        for g in range(nf):
            dense = wb[g, b].astype(F32)
            for r in range(rows):
                wf[pl.ds(g * rows + r, tiles, stride=nf * rows), :] = dense[r * tiles : (r + 1) * tiles]
        for j in range(tiles):
            here = pl.ds(pl.multiple_of(b * block + j * LANES, LANES), LANES)
            fw[:, here] = wf[pl.ds(j * nf * rows, nf * rows), :].astype(BF16)
        return carry

    lax.fori_loop(0, NY, place_weights, 0)

    drain(ra.at[pl.ds(0, NY - 1)], a_sem.at[0])
    drain(zb.at[pl.ds(0, nz - 1)], b_sem.at[0])
    for k in range(ITERS):
        drain(xs.at[k, pl.ds(0, nf - 1)], x_sem.at[k, 0])
        drain(ys.at[k, pl.ds(0, NY - 1)], y_sem.at[k, 0])
        drain(zs.at[k, pl.ds(0, nz - 1)], z_sem.at[k, 0])
    drain(cd.at[0, pl.ds(0, nz - 1)], cz_sem.at[0])
    drain(cd.at[pl.ds(0, NY - 1)], cy_send.at[0])
    drain(wb.at[pl.ds(0, nf - 1)], w_send.at[0])


def solution(mesh):
    nf, nz = mesh.shape["fsdp"], mesh.shape["rep"] // NY

    def body(deltas, momentum, master):
        _, rows, width = deltas.shape
        block = width // NY
        chunk = block * rows // nz
        parts, tiles = chunk // LANES, block // LANES
        vmem = pl.BlockSpec(memory_space=pltpu.VMEM)
        dma = pltpu.SemaphoreType.DMA
        return pl.pallas_call(
            functools.partial(kernel, nf, nz),
            out_shape=(
                jax.ShapeDtypeStruct((rows, width), F32),
                jax.ShapeDtypeStruct((rows, width), F32),
                jax.ShapeDtypeStruct((nf * rows, width), BF16),
            ),
            in_specs=[pl.BlockSpec(memory_space=pl.ANY), vmem, vmem],
            out_specs=(vmem, vmem, vmem),
            scratch_shapes=[
                pltpu.VMEM((rows, width), BF16),
                pltpu.VMEM((NY, rows, block), BF16),
                pltpu.VMEM((tiles * NY * 8, LANES), F32),
                pltpu.VMEM((rows, NY, block), BF16),
                pltpu.VMEM((nz, NY, chunk), BF16),
                pltpu.VMEM((LANES, LANES), F32),
                pltpu.VMEM((ITERS, nf, 1, LANES), F32),
                pltpu.VMEM((ITERS, NY, 1, LANES), F32),
                pltpu.VMEM((ITERS, nz, 1, LANES), F32),
                pltpu.VMEM((NY, nz, parts, LANES), F32),
                pltpu.VMEM((rows * tiles, LANES), F32),
                pltpu.VMEM((rows * tiles, LANES), F32),
                pltpu.VMEM((nf, NY, rows * tiles, LANES), BF16),
                pltpu.VMEM((tiles * nf * rows, LANES), F32),
                dma((2,)),
                dma((2,)),
                dma((2,)),
                dma((ITERS, 2)),
                dma((ITERS, 2)),
                dma((ITERS, 2)),
                dma((2,)),
                dma((1,)),
                dma((NY,)),
                dma((1,)),
                dma((NY,)),
            ],
            compiler_params=pltpu.CompilerParams(collective_id=0, has_side_effects=True),
        )(deltas, momentum, master)

    placed = (P("rep", "fsdp", None), P("fsdp", None), P("fsdp", None))
    return jax.shard_map(
        body,
        mesh=mesh,
        in_specs=placed,
        out_specs=(P("fsdp", None), P("fsdp", None), P()),
        check_vma=False,
    )
```

```python
import functools

import jax
import jax.numpy as jnp
from jax import lax
from jax.experimental import pallas as pl
from jax.experimental.pallas import tpu as pltpu
from jax.sharding import PartitionSpec as P

ITERS = 3
EPS = 1e-06
NY = 8
LANES = 128
MESH = pl.DeviceIdType.MESH
F32, BF16 = jnp.float32, jnp.bfloat16


def split3(value):
    high = value.astype(BF16)
    rest = value - high.astype(F32)
    mid = rest.astype(BF16)
    low = (rest - mid.astype(F32)).astype(BF16)
    return high, mid, low


def kernel(
    nf, nz, delta, mom_in, mas_in, nm_out, ns_out, fw_out,
    own, mom, mas, nm, ns, fw, ra, rf, tb, zb, zq, ps, zs, cd, cn, nd, wb, wf,
    local_sem, out_sem, a_sem, b_sem, p_sem, z_sem, cz_sem, cy_send, cy_recv, w_send, w_recv, v_send, v_recv,
):
    rows, width = own.shape
    block = width // NY
    halves = nz // rows
    chunk = block // halves
    tiles = block // LANES
    parts = chunk // LANES
    reps = NY * nz
    entries = nf * rows * width

    rep, f = lax.axis_index("rep"), lax.axis_index("fsdp")
    y, z = lax.rem(rep, NY), lax.div(rep, NY)

    x, core = lax.div(f, 2), lax.rem(f, 2)
    plane = y * nf + f
    sibling = (rep, f + 1 - 2 * core)

    def peers(axis, visit):
        n = {"x": nf // 2, "y": NY, "z": nz, "plane": NY * nf}[axis]
        me = {"x": x, "y": y, "z": z, "plane": plane}[axis]

        def step(i, carry):
            half = lax.div(i + 1, 2)
            place = lax.rem(me + n // 2 + half * (2 * lax.rem(i, 2) - 1) + n, n)
            if axis == "x":
                device = (rep, 2 * place + core)
            elif axis == "y":
                device = (z * NY + place, f)
            elif axis == "z":
                device = (place * NY + y, f)
            else:
                device = (z * NY + lax.div(place, nf), lax.rem(place, nf))
            visit(device, place)
            return carry

        lax.fori_loop(0, n - 1, step, 0)

    def send(src, dst, send_sem, recv_sem, device):
        pltpu.make_async_remote_copy(
            src_ref=src, dst_ref=dst, send_sem=send_sem, recv_sem=recv_sem,
            device_id=device, device_id_type=MESH,
        ).start()

    def drain(ref, sem):
        pltpu.make_async_copy(ref, ref, sem).wait()

    own_copy = pltpu.make_async_copy(delta.at[0], own, local_sem.at[0])
    own_copy.start()
    mine = pl.ds(pl.multiple_of(y * block, block), block)
    block_copy = pltpu.make_async_copy(delta.at[0, :, mine], ra.at[y], local_sem.at[1])
    block_copy.start()

    barrier = pltpu.get_barrier_semaphore()

    def greet(device, place):
        pl.semaphore_signal(barrier, inc=1, device_id=device, device_id_type=MESH)

    peers("plane", greet)
    peers("z", greet)

    mom_copy = pltpu.make_async_copy(mom_in, mom, local_sem.at[2])
    mas_copy = pltpu.make_async_copy(mas_in, mas, local_sem.at[3])
    lane = lax.broadcasted_iota(jnp.int32, (1, LANES), 1)
    own_copy.wait()
    value = own[...].astype(F32)
    squared = jnp.sum(jnp.sum(value * value, axis=0, keepdims=True), axis=1, keepdims=True)
    row = jnp.where(lane == rep, squared, 0.0)
    pl.semaphore_wait(barrier, NY * nf + nz - 2)

    def send_a(device, place):
        columns = pl.ds(pl.multiple_of(place * block, block), block)
        send(own.at[:, columns], ra.at[y], a_sem.at[0], a_sem.at[1], device)

    def exchange(axis, n, me, buffer, sems, row):
        buffer[me] = row
        peers(axis, lambda device, place: send(buffer.at[me], buffer.at[me], sems.at[0], sems.at[1], device))

        def total():
            drain(buffer.at[pl.ds(0, n - 1)], sems.at[1])
            return jnp.sum(buffer[...], axis=0)

        return total

    def plane_stage(k, row):
        return exchange("plane", NY * nf, plane, ps.at[k], p_sem.at[k], row)

    def z_stage(k, row):
        return exchange("z", nz, z, zs.at[k], z_sem.at[k], row)

    peers("y", send_a)
    total = plane_stage(0, row)
    mom_copy.start()
    mas_copy.start()

    block_copy.wait()
    drain(ra.at[pl.ds(0, NY - 1)], a_sem.at[1])
    for k in range(NY):
        arrived = ra[k].astype(F32)
        for j in range(tiles):
            rf[pl.ds(8 * (j * NY + k), rows), :] = arrived[:, j * LANES : (j + 1) * LANES]
    for r in range(rows):
        for j in range(tiles):
            column = pl.ds(j * LANES, LANES)
            tb[r, :, column] = rf[pl.ds(8 * j * NY + r, NY, stride=8), :].astype(BF16)

    def piece(place):
        columns = pl.ds(pl.multiple_of(lax.rem(place, halves) * chunk, chunk), chunk)
        return tb.at[lax.div(place, halves), :, columns]

    peers("z", lambda device, place: send(piece(place), zb.at[z], b_sem.at[0], b_sem.at[1], device))
    total = z_stage(0, total())
    zb[z] = piece(z)[...]
    zq[pl.ds(reps, LANES - reps), :] = jnp.zeros((LANES - reps, LANES), F32)

    row = total()
    drain(zb.at[pl.ds(0, nz - 1)], b_sem.at[1])
    held = zb[...].reshape(reps, chunk)

    def center_of(squared):
        weight = jnp.where(lane < reps, 1.0 / jnp.sqrt(squared / entries + EPS), 0.0)
        share = weight / jnp.sum(weight, axis=1, keepdims=True)
        left = jnp.concatenate(split3(share), axis=0)[:, :reps]
        return jnp.sum(jnp.dot(left, held, preferred_element_type=F32), axis=0, keepdims=True)

    def iterate(k, center):
        spread = held.astype(F32) - center
        spread = spread * spread
        partial = spread[:, :LANES]
        for part in range(1, parts):
            partial = partial + spread[:, part * LANES : (part + 1) * LANES]
        zq[pl.ds(0, reps), :] = partial
        row = lax.dot_general(
            jnp.ones((8, LANES), F32), zq[...], (((1,), (1,)), ((), ())),
            precision=lax.Precision.HIGHEST, preferred_element_type=F32,
        )[:1]
        return center_of(z_stage(k, plane_stage(k, row)())())

    center = lax.fori_loop(1, ITERS, iterate, center_of(row))

    for part in range(parts):
        cd[y, z, pl.ds(part, 1), :] = center[:, part * LANES : (part + 1) * LANES]
    peers("z", lambda device, place: send(cd.at[y, z], cd.at[y, z], cz_sem.at[0], cz_sem.at[1], device))
    mom_copy.wait()
    mas_copy.wait()
    drain(cd.at[0, pl.ds(0, nz - 1)], cz_sem.at[1])
    peers("y", lambda device, place: send(cd.at[y], cd.at[y], cy_send.at[0], cy_recv.at[y], device))

    def nearest(i):
        half = lax.div(i, 2) + lax.rem(i, 2)
        return lax.rem(y + half * (1 - 2 * lax.rem(i, 2)) + NY, NY)

    def out_copies(b):
        columns = pl.ds(pl.multiple_of(b * block, block), block)
        return [
            pltpu.make_async_copy(ref.at[:, columns], out.at[:, columns], out_sem.at[at, b])
            for at, (ref, out) in enumerate(((nm, nm_out), (ns, ns_out), (fw, fw_out)))
        ]

    def update(i, carry):
        b = nearest(i)

        @pl.when(i > 0)
        def _():
            drain(cd.at[b], cy_recv.at[b])

        for k in range(nz):
            cn[pl.ds(k * parts, parts), :] = cd[b, k]
        for j in range(tiles):
            here = pl.ds(pl.multiple_of(b * block + j * LANES, LANES), LANES)
            there = pl.ds(j, rows, stride=tiles)
            c = cn[there, :]
            momentum = 0.9 * mom[:, here] + c
            master = mas[:, here] - 0.7 * (c + 0.9 * momentum)
            nm[:, here] = momentum
            ns[:, here] = master
            nd[there, :] = master
        wb[f, b] = nd[...].astype(BF16)
        peers("x", lambda device, place: send(wb.at[f, b], wb.at[f, b], w_send.at[0], w_recv.at[b], device))
        send(wb.at[f, b], wb.at[f, b], v_send.at[0], v_recv.at[b], sibling)
        for copy in out_copies(b)[:2]:
            copy.start()
        return carry

    lax.fori_loop(0, NY, update, 0)

    def forward(i, carry):
        b = nearest(i)
        drain(wb.at[pl.ds(0, nf // 2 - 1), b], w_recv.at[b])

        def step(k, carry):
            g = 2 * lax.rem(x + 1 + k, nf // 2) + core
            send(wb.at[g, b], wb.at[g, b], v_send.at[0], v_recv.at[b], sibling)
            return carry

        return lax.fori_loop(0, nf // 2 - 1, step, carry)

    lax.fori_loop(0, NY, forward, 0)

    def place_weights(i, carry):
        b = nearest(i)
        drain(wb.at[pl.ds(0, nf // 2), b], v_recv.at[b])
        for g in range(nf):
            dense = wb[g, b].astype(F32)
            for r in range(rows):
                wf[pl.ds(g * rows + r, tiles, stride=nf * rows), :] = dense[r * tiles : (r + 1) * tiles]
        for j in range(tiles):
            here = pl.ds(pl.multiple_of(b * block + j * LANES, LANES), LANES)
            fw[:, here] = wf[pl.ds(j * nf * rows, nf * rows), :].astype(BF16)
        out_copies(b)[2].start()
        return carry

    lax.fori_loop(0, NY, place_weights, 0)

    def leave(i, carry):
        for copy in out_copies(i):
            copy.wait()
        return carry

    lax.fori_loop(0, NY, leave, 0)
    drain(ra.at[pl.ds(0, NY - 1)], a_sem.at[0])
    drain(zb.at[pl.ds(0, nz - 1)], b_sem.at[0])
    for k in range(ITERS):
        drain(ps.at[k, pl.ds(0, NY * nf - 1)], p_sem.at[k, 0])
        drain(zs.at[k, pl.ds(0, nz - 1)], z_sem.at[k, 0])
    drain(cd.at[0, pl.ds(0, nz - 1)], cz_sem.at[0])
    drain(cd.at[pl.ds(0, NY - 1)], cy_send.at[0])
    drain(wb.at[pl.ds(0, nf // 2 - 1)], w_send.at[0])
    drain(wb.at[pl.ds(0, nf // 2)], v_send.at[0])


def copy_kernel(count, *refs):
    sems = refs[-1]
    copies = [pltpu.make_async_copy(refs[i], refs[count + i], sems.at[i]) for i in range(count)]
    for copy in copies:
        copy.start()
    for copy in copies:
        copy.wait()


def solution(mesh):
    nf, nz = mesh.shape["fsdp"], mesh.shape["rep"] // NY

    def body(deltas, momentum, master):
        _, rows, width = deltas.shape
        block = width // NY
        chunk = block * rows // nz
        parts, tiles = chunk // LANES, block // LANES
        anywhere = pl.BlockSpec(memory_space=pl.ANY)
        dma = pltpu.SemaphoreType.DMA
        outs = (
            jax.ShapeDtypeStruct((rows, width), F32),
            jax.ShapeDtypeStruct((rows, width), F32),
            jax.ShapeDtypeStruct((nf * rows, width), BF16),
        )
        results = pl.pallas_call(
            functools.partial(kernel, nf, nz),
            out_shape=outs,
            in_specs=[pl.BlockSpec(memory_space=pltpu.HBM)] * 3,
            out_specs=(anywhere,) * 3,
            scratch_shapes=[
                pltpu.VMEM((rows, width), BF16),
                pltpu.VMEM((rows, width), F32),
                pltpu.VMEM((rows, width), F32),
                pltpu.VMEM((rows, width), F32),
                pltpu.VMEM((rows, width), F32),
                pltpu.VMEM((nf * rows, width), BF16),
                pltpu.VMEM((NY, rows, block), BF16),
                pltpu.VMEM((tiles * NY * 8, LANES), F32),
                pltpu.VMEM((rows, NY, block), BF16),
                pltpu.VMEM((nz, NY, chunk), BF16),
                pltpu.VMEM((LANES, LANES), F32),
                pltpu.VMEM((ITERS, NY * nf, 1, LANES), F32),
                pltpu.VMEM((ITERS, nz, 1, LANES), F32),
                pltpu.VMEM((NY, nz, parts, LANES), F32),
                pltpu.VMEM((rows * tiles, LANES), F32),
                pltpu.VMEM((rows * tiles, LANES), F32),
                pltpu.VMEM((nf, NY, rows * tiles, LANES), BF16),
                pltpu.VMEM((tiles * nf * rows, LANES), F32),
                dma((4,)),
                dma((3, NY)),
                dma((2,)),
                dma((2,)),
                dma((ITERS, 2)),
                dma((ITERS, 2)),
                dma((2,)),
                dma((1,)),
                dma((NY,)),
                dma((1,)),
                dma((NY,)),
                dma((1,)),
                dma((NY,)),
            ],
            compiler_params=pltpu.CompilerParams(
                collective_id=0, has_side_effects=True, vmem_limit_bytes=16 * 2**20
            ),
        )(deltas, momentum, master)
        return pl.pallas_call(
            functools.partial(copy_kernel, len(outs)),
            out_shape=outs,
            in_specs=[pl.BlockSpec(memory_space=pltpu.VMEM)] * len(outs),
            out_specs=(anywhere,) * len(outs),
            scratch_shapes=[dma((len(outs),))],
            compiler_params=pltpu.CompilerParams(vmem_limit_bytes=16 * 2**20),
        )(*results)

    placed = (P("rep", "fsdp", None), P("fsdp", None), P("fsdp", None))
    return jax.shard_map(
        body,
        mesh=mesh,
        in_specs=placed,
        out_specs=(P("fsdp", None), P("fsdp", None), P()),
        check_vma=False,
    )
```

```python
import functools

import jax
import jax.numpy as jnp
from jax import lax
from jax.experimental import pallas as pl
from jax.experimental.pallas import tpu as pltpu
from jax.sharding import PartitionSpec as P

EPS = 1e-06
NY = 8
LANES = 128
MESH = pl.DeviceIdType.MESH
F32, BF16 = jnp.float32, jnp.bfloat16


def split3(value):
    high = value.astype(BF16)
    rest = value - high.astype(F32)
    mid = rest.astype(BF16)
    low = (rest - mid.astype(F32)).astype(BF16)
    return high, mid, low


def kernel(
    nf, nz, delta, mom_in, mas_in, nm_out, ns_out, fw_out,
    own, mom, mas, nm, ns, fw, ra, rf, tb, zb, ps, zs, gm, gc, gs, gx, gy, gz, gf, gt, cd, cn, nd, wb, wf,
    local_sem, out_sem, a_sem, b_sem, p_sem, z_sem, gc_sem, gx_sem, gy_sem, gz_sem, gf_sem, cz_send, cz_recv, cy_send, cy_recv, w_send, w_recv, v_send, v_recv,
):
    rows, width = own.shape
    block = width // NY
    halves = nz // rows
    chunk = block // halves
    tiles = block // LANES
    parts = chunk // LANES
    reps = NY * nz
    entries = nf * rows * width

    rep, f = lax.axis_index("rep"), lax.axis_index("fsdp")
    y, z = lax.rem(rep, NY), lax.div(rep, NY)

    x, core = lax.div(f, 2), lax.rem(f, 2)
    plane = y * nf + f
    sibling = (rep, f + 1 - 2 * core)

    def peers(axis, visit):
        n = {"x": nf // 2, "f": nf, "y": NY, "z": nz, "plane": NY * nf}[axis]
        me = {"x": x, "f": f, "y": y, "z": z, "plane": plane}[axis]

        def step(i, carry):
            half = lax.div(i + 1, 2)
            place = lax.rem(me + n // 2 + half * (2 * lax.rem(i, 2) - 1) + n, n)
            if axis == "x":
                device = (rep, 2 * place + core)
            elif axis == "f":
                device = (rep, place)
            elif axis == "y":
                device = (z * NY + place, f)
            elif axis == "z":
                device = (place * NY + y, f)
            else:
                device = (z * NY + lax.div(place, nf), lax.rem(place, nf))
            visit(device, place)
            return carry

        lax.fori_loop(0, n - 1, step, 0)

    def send(src, dst, send_sem, recv_sem, device):
        pltpu.make_async_remote_copy(
            src_ref=src, dst_ref=dst, send_sem=send_sem, recv_sem=recv_sem,
            device_id=device, device_id_type=MESH,
        ).start()

    def drain(ref, sem):
        pltpu.make_async_copy(ref, ref, sem).wait()

    own_copy = pltpu.make_async_copy(delta.at[0], own, local_sem.at[0])
    own_copy.start()
    mine = pl.ds(pl.multiple_of(y * block, block), block)
    block_copy = pltpu.make_async_copy(delta.at[0, :, mine], ra.at[y], local_sem.at[1])
    block_copy.start()

    barrier = pltpu.get_barrier_semaphore()

    def greet(device, place):
        pl.semaphore_signal(barrier, inc=1, device_id=device, device_id_type=MESH)

    peers("plane", greet)
    peers("z", greet)

    mom_copy = pltpu.make_async_copy(mom_in, mom, local_sem.at[2])
    mas_copy = pltpu.make_async_copy(mas_in, mas, local_sem.at[3])
    lane = lax.broadcasted_iota(jnp.int32, (1, LANES), 1)
    own_copy.wait()
    value = own[...].astype(F32)
    squared = jnp.sum(jnp.sum(value * value, axis=0, keepdims=True), axis=1, keepdims=True)
    row = jnp.where(lane == rep, squared, 0.0)
    pl.semaphore_wait(barrier, NY * nf + nz - 2)

    def send_a(device, place):
        columns = pl.ds(pl.multiple_of(place * block, block), block)
        send(own.at[:, columns], ra.at[y], a_sem.at[0], a_sem.at[1], device)

    def exchange(axis, n, me, buffer, sems, row):
        buffer[me] = row
        peers(axis, lambda device, place: send(buffer.at[me], buffer.at[me], sems.at[0], sems.at[1], device))

        def total():
            drain(buffer.at[pl.ds(0, n - 1)], sems.at[1])
            return jnp.sum(buffer[...], axis=0)

        return total

    peers("y", send_a)
    total = exchange("plane", NY * nf, plane, ps, p_sem, row)
    mom_copy.start()
    mas_copy.start()

    block_copy.wait()
    drain(ra.at[pl.ds(0, NY - 1)], a_sem.at[1])
    for k in range(NY):
        arrived = ra[k].astype(F32)
        for j in range(tiles):
            rf[pl.ds(8 * (j * NY + k), rows), :] = arrived[:, j * LANES : (j + 1) * LANES]
    for r in range(rows):
        for j in range(tiles):
            column = pl.ds(j * LANES, LANES)
            tb[r, :, column] = rf[pl.ds(8 * j * NY + r, NY, stride=8), :].astype(BF16)

    def piece(place):
        columns = pl.ds(pl.multiple_of(lax.rem(place, halves) * chunk, chunk), chunk)
        return tb.at[lax.div(place, halves), :, columns]

    peers("z", lambda device, place: send(piece(place), zb.at[z], b_sem.at[0], b_sem.at[1], device))
    total = exchange("z", nz, z, zs, z_sem, total())
    zb[z] = piece(z)[...]

    row = total()
    drain(zb.at[pl.ds(0, nz - 1)], b_sem.at[1])
    held = zb[...].reshape(reps, chunk)

    def shares(squared):
        weight = jnp.where(lane < reps, 1.0 / jnp.sqrt(squared / entries + EPS), 0.0)
        return weight / jnp.sum(weight, axis=1, keepdims=True)

    def center_of(share):
        left = jnp.concatenate(split3(share), axis=0)[:, :reps]
        return jnp.sum(jnp.dot(left, held, preferred_element_type=F32), axis=0, keepdims=True)

    half = reps // 2
    spread = held.astype(F32) - center_of(shares(row))
    first, second = spread[:half], spread[half:]
    blank = jnp.zeros((LANES - reps, chunk), F32)

    def products(left, *right):
        return lax.dot_general(
            left, jnp.concatenate((*right, blank), axis=0), (((1,), (1,)), ((), ())),
            precision=lax.Precision.HIGHEST, preferred_element_type=F32,
        )

    at_row = lax.broadcasted_iota(jnp.int32, (half, LANES), 0)
    at_lane = lax.broadcasted_iota(jnp.int32, (half, LANES), 1)
    upper, lower = products(first, second, first), products(second, first, second)
    ends = jnp.sum(jnp.where(at_lane - half == at_row, lower, 0.0), axis=1, keepdims=True)
    kept = jnp.where((at_lane < half) | (at_lane - half >= at_row), upper, lower)
    kept = jnp.where(at_lane < reps, kept, jnp.where(at_lane == reps, ends, 0.0))

    share_rows = half // nf
    for g in range(nf):
        gm[g % 2, g // 2] = kept[g * share_rows : (g + 1) * share_rows]
    send(gm.at[1 - core], gc, gc_sem.at[0], gc_sem.at[1], sibling)
    drain(gc, gc_sem.at[1])
    gs[...] = gm[core] + gc[...]
    gx[x] = gs[x]
    peers("x", lambda device, place: send(gs.at[place], gx.at[x], gx_sem.at[0], gx_sem.at[1], device))
    drain(gx.at[pl.ds(0, nf // 2 - 1)], gx_sem.at[1])
    piece_sum = jnp.sum(gx[...], axis=0)
    piece_sum = exchange("y", NY, y, gy, gy_sem, piece_sum)()
    piece_sum = exchange("z", nz, z, gz, gz_sem, piece_sum)()
    gf[f] = piece_sum
    peers("f", lambda device, place: send(gf.at[f], gf.at[f], gf_sem.at[0], gf_sem.at[1], device))
    drain(gf.at[pl.ds(0, nf - 1)], gf_sem.at[1])
    for g in range(nf):
        gt[pl.ds(g * share_rows, share_rows), :] = gf[g]

    kept = gt[...]
    same = at_lane == at_row

    def to_row(column):
        return jnp.sum(jnp.where(same, column, 0.0), axis=0, keepdims=True)

    def to_column(line):
        return jnp.sum(jnp.where(same, line, 0.0), axis=1, keepdims=True)

    mixed = pltpu.roll(kept, LANES - half, 1)
    between = jnp.where(at_lane < half, kept, 0.0)
    upper = jnp.where((at_lane < half) & (at_lane >= at_row), mixed, 0.0)
    lower = jnp.where(at_lane < at_row, mixed, 0.0)
    ends_first = jnp.sum(jnp.where(same, mixed, 0.0), axis=0, keepdims=True)
    ends_second = to_row(kept[:, reps : reps + 1])
    squared = ends_first + pltpu.roll(ends_second, half, 1)
    share = shares(squared)
    share_first = jnp.where(lane < half, share, 0.0)
    share_second = jnp.where(lane < half, pltpu.roll(share, LANES - half, 1), 0.0)
    column_first, column_second = to_column(share_first), to_column(share_second)
    with_first = (
        jnp.sum(upper * column_first, axis=0, keepdims=True)
        + to_row(jnp.sum(upper * share_first + between * share_second, axis=1, keepdims=True))
        - ends_first * share_first
    )
    with_second = (
        jnp.sum(between * column_first + lower * column_second, axis=0, keepdims=True)
        + to_row(jnp.sum(lower * share_second, axis=1, keepdims=True))
        + ends_second * share_second
    )
    along = with_first + pltpu.roll(with_second, half, 1)
    squared = squared - 2.0 * along + jnp.sum(share * along, axis=1, keepdims=True)
    center = center_of(shares(jnp.maximum(squared, 0.0)))

    for part in range(parts):
        cd[y, z, pl.ds(part, 1), :] = center[:, part * LANES : (part + 1) * LANES]
    peers("z", lambda device, place: send(cd.at[y, z], cd.at[y, z], cz_send.at[0], cz_recv.at[z], device))

    def pass_on(i, carry):
        half = lax.div(i, 2) + lax.rem(i, 2)
        g = lax.rem(z + half * (1 - 2 * lax.rem(i, 2)) + nz, nz)

        @pl.when(i > 0)
        def _():
            drain(cd.at[0, g], cz_recv.at[g])

        peers("y", lambda device, place: send(cd.at[y, g], cd.at[y, g], cy_send.at[0], cy_recv.at[y], device))
        return carry

    lax.fori_loop(0, nz, pass_on, 0)
    mom_copy.wait()
    mas_copy.wait()

    def nearest(i):
        half = lax.div(i, 2) + lax.rem(i, 2)
        return lax.rem(y + half * (1 - 2 * lax.rem(i, 2)) + NY, NY)

    def out_copies(b):
        columns = pl.ds(pl.multiple_of(b * block, block), block)
        return [
            pltpu.make_async_copy(ref.at[:, columns], out.at[:, columns], out_sem.at[at, b])
            for at, (ref, out) in enumerate(((nm, nm_out), (ns, ns_out), (fw, fw_out)))
        ]

    def update(i, carry):
        b = nearest(i)

        @pl.when(i > 0)
        def _():
            drain(cd.at[b], cy_recv.at[b])

        for k in range(nz):
            cn[pl.ds(k * parts, parts), :] = cd[b, k]
        for j in range(tiles):
            here = pl.ds(pl.multiple_of(b * block + j * LANES, LANES), LANES)
            there = pl.ds(j, rows, stride=tiles)
            c = cn[there, :]
            momentum = 0.9 * mom[:, here] + c
            master = mas[:, here] - 0.7 * (c + 0.9 * momentum)
            nm[:, here] = momentum
            ns[:, here] = master
            nd[there, :] = master
        wb[f, b] = nd[...].astype(BF16)
        peers("x", lambda device, place: send(wb.at[f, b], wb.at[f, b], w_send.at[0], w_recv.at[b], device))
        send(wb.at[f, b], wb.at[f, b], v_send.at[0], v_recv.at[b], sibling)
        for copy in out_copies(b)[:2]:
            copy.start()
        return carry

    lax.fori_loop(0, NY, update, 0)

    def forward(i, carry):
        b = nearest(i)
        drain(wb.at[pl.ds(0, nf // 2 - 1), b], w_recv.at[b])

        def step(k, carry):
            g = 2 * lax.rem(x + 1 + k, nf // 2) + core
            send(wb.at[g, b], wb.at[g, b], v_send.at[0], v_recv.at[b], sibling)
            return carry

        return lax.fori_loop(0, nf // 2 - 1, step, carry)

    lax.fori_loop(0, NY, forward, 0)

    def place_weights(i, carry):
        b = nearest(i)
        drain(wb.at[pl.ds(0, nf // 2), b], v_recv.at[b])
        for g in range(nf):
            dense = wb[g, b].astype(F32)
            for r in range(rows):
                wf[pl.ds(g * rows + r, tiles, stride=nf * rows), :] = dense[r * tiles : (r + 1) * tiles]
        for j in range(tiles):
            here = pl.ds(pl.multiple_of(b * block + j * LANES, LANES), LANES)
            fw[:, here] = wf[pl.ds(j * nf * rows, nf * rows), :].astype(BF16)
        out_copies(b)[2].start()
        return carry

    lax.fori_loop(0, NY, place_weights, 0)

    def leave(i, carry):
        for copy in out_copies(i):
            copy.wait()
        return carry

    lax.fori_loop(0, NY, leave, 0)
    drain(ra.at[pl.ds(0, NY - 1)], a_sem.at[0])
    drain(zb.at[pl.ds(0, nz - 1)], b_sem.at[0])
    drain(ps.at[pl.ds(0, NY * nf - 1)], p_sem.at[0])
    drain(zs.at[pl.ds(0, nz - 1)], z_sem.at[0])
    drain(gc, gc_sem.at[0])
    drain(gx.at[pl.ds(0, nf // 2 - 1)], gx_sem.at[0])
    drain(gy.at[pl.ds(0, NY - 1)], gy_sem.at[0])
    drain(gz.at[pl.ds(0, nz - 1)], gz_sem.at[0])
    drain(gf.at[pl.ds(0, nf - 1)], gf_sem.at[0])
    drain(cd.at[0, pl.ds(0, nz - 1)], cz_send.at[0])
    drain(cd.at[pl.ds(0, NY - 1)], cy_send.at[0])
    drain(wb.at[pl.ds(0, nf // 2 - 1)], w_send.at[0])
    drain(wb.at[pl.ds(0, nf // 2)], v_send.at[0])


def copy_kernel(count, *refs):
    sems = refs[-1]
    copies = [pltpu.make_async_copy(refs[i], refs[count + i], sems.at[i]) for i in range(count)]
    for copy in copies:
        copy.start()
    for copy in copies:
        copy.wait()


def solution(mesh):
    nf, nz = mesh.shape["fsdp"], mesh.shape["rep"] // NY

    def body(deltas, momentum, master):
        _, rows, width = deltas.shape
        block = width // NY
        chunk = block * rows // nz
        parts, tiles = chunk // LANES, block // LANES
        share_rows = NY * nz // 2 // nf
        anywhere = pl.BlockSpec(memory_space=pl.ANY)
        dma = pltpu.SemaphoreType.DMA
        outs = (
            jax.ShapeDtypeStruct((rows, width), F32),
            jax.ShapeDtypeStruct((rows, width), F32),
            jax.ShapeDtypeStruct((nf * rows, width), BF16),
        )
        results = pl.pallas_call(
            functools.partial(kernel, nf, nz),
            out_shape=outs,
            in_specs=[pl.BlockSpec(memory_space=pltpu.HBM)] * 3,
            out_specs=(anywhere,) * 3,
            scratch_shapes=[
                pltpu.VMEM((rows, width), BF16),
                pltpu.VMEM((rows, width), F32),
                pltpu.VMEM((rows, width), F32),
                pltpu.VMEM((rows, width), F32),
                pltpu.VMEM((rows, width), F32),
                pltpu.VMEM((nf * rows, width), BF16),
                pltpu.VMEM((NY, rows, block), BF16),
                pltpu.VMEM((tiles * NY * 8, LANES), F32),
                pltpu.VMEM((rows, NY, block), BF16),
                pltpu.VMEM((nz, NY, chunk), BF16),
                pltpu.VMEM((NY * nf, 1, LANES), F32),
                pltpu.VMEM((nz, 1, LANES), F32),
                pltpu.VMEM((2, nf // 2, share_rows, LANES), F32),
                pltpu.VMEM((nf // 2, share_rows, LANES), F32),
                pltpu.VMEM((nf // 2, share_rows, LANES), F32),
                pltpu.VMEM((nf // 2, share_rows, LANES), F32),
                pltpu.VMEM((NY, share_rows, LANES), F32),
                pltpu.VMEM((nz, share_rows, LANES), F32),
                pltpu.VMEM((nf, share_rows, LANES), F32),
                pltpu.VMEM((nf * share_rows, LANES), F32),
                pltpu.VMEM((NY, nz, parts, LANES), F32),
                pltpu.VMEM((rows * tiles, LANES), F32),
                pltpu.VMEM((rows * tiles, LANES), F32),
                pltpu.VMEM((nf, NY, rows * tiles, LANES), BF16),
                pltpu.VMEM((tiles * nf * rows, LANES), F32),
                dma((4,)),
                dma((3, NY)),
                dma((2,)),
                dma((2,)),
                dma((2,)),
                dma((2,)),
                dma((2,)),
                dma((2,)),
                dma((2,)),
                dma((2,)),
                dma((2,)),
                dma((1,)),
                dma((nz,)),
                dma((1,)),
                dma((NY,)),
                dma((1,)),
                dma((NY,)),
                dma((1,)),
                dma((NY,)),
            ],
            compiler_params=pltpu.CompilerParams(
                collective_id=0, has_side_effects=True, vmem_limit_bytes=16 * 2**20
            ),
        )(*(pltpu.with_memory_space_constraint(value, pltpu.HBM) for value in (deltas, momentum, master)))
        return pl.pallas_call(
            functools.partial(copy_kernel, len(outs)),
            out_shape=outs,
            in_specs=[pl.BlockSpec(memory_space=pltpu.VMEM)] * len(outs),
            out_specs=(anywhere,) * len(outs),
            scratch_shapes=[dma((len(outs),))],
            compiler_params=pltpu.CompilerParams(vmem_limit_bytes=16 * 2**20),
        )(*results)

    placed = (P("rep", "fsdp", None), P("fsdp", None), P("fsdp", None))
    return jax.shard_map(
        body,
        mesh=mesh,
        in_specs=placed,
        out_specs=(P("fsdp", None), P("fsdp", None), P()),
        check_vma=False,
    )
```

```python
import functools

import jax
import jax.numpy as jnp
from jax import lax
from jax.experimental import pallas as pl
from jax.experimental.pallas import tpu as pltpu
from jax.sharding import PartitionSpec as P

EPS = 1e-06
NY = 8
LANES = 128
MESH = pl.DeviceIdType.MESH
F32, BF16 = jnp.float32, jnp.bfloat16


def split3(value):
    high = value.astype(BF16)
    rest = value - high.astype(F32)
    mid = rest.astype(BF16)
    low = (rest - mid.astype(F32)).astype(BF16)
    return high, mid, low


def kernel(
    nf, nz, delta, mom_in, mas_in, nm_out, ns_out, fw_out,
    own, mom, mas, nm, ns, fw, ra, rf, tb, zb, fs, ys, zs, gm, gx, gy, gz, gf, gt, cd, cn, nd, wb, wf,
    local_sem, out_sem, a_sem, b_sem, f_sem, y_sem, z_sem, gx_sem, gy_sem, gz_sem, gf_sem, cz_send, cz_recv, cy_send, cy_recv, w_send, w_recv, v_send, v_recv,
):
    rows, width = own.shape
    block = width // NY
    halves = nz // rows
    chunk = block // halves
    tiles = block // LANES
    parts = chunk // LANES
    reps = NY * nz
    entries = nf * rows * width

    rep, f = lax.axis_index("rep"), lax.axis_index("fsdp")
    y, z = lax.rem(rep, NY), lax.div(rep, NY)

    x, core = lax.div(f, 2), lax.rem(f, 2)
    sibling = (rep, f + 1 - 2 * core)

    def peers(axis, visit):
        n = {"x": nf // 2, "f": nf, "y": NY, "z": nz}[axis]
        me = {"x": x, "f": f, "y": y, "z": z}[axis]

        def step(i, carry):
            half = lax.div(i + 1, 2)
            place = lax.rem(me + n // 2 + half * (2 * lax.rem(i, 2) - 1) + n, n)
            if axis == "x":
                device = (rep, 2 * place + core)
            elif axis == "f":
                device = (rep, place)
            elif axis == "y":
                device = (z * NY + place, f)
            else:
                device = (place * NY + y, f)
            visit(device, place)
            return carry

        lax.fori_loop(0, n - 1, step, 0)

    def send(src, dst, send_sem, recv_sem, device):
        pltpu.make_async_remote_copy(
            src_ref=src, dst_ref=dst, send_sem=send_sem, recv_sem=recv_sem,
            device_id=device, device_id_type=MESH,
        ).start()

    def drain(ref, sem):
        pltpu.make_async_copy(ref, ref, sem).wait()

    own_copy = pltpu.make_async_copy(delta.at[0], own, local_sem.at[0])
    own_copy.start()
    mine = pl.ds(pl.multiple_of(y * block, block), block)
    block_copy = pltpu.make_async_copy(delta.at[0, :, mine], ra.at[y], local_sem.at[1])
    block_copy.start()

    barrier = pltpu.get_barrier_semaphore()

    def greet(device, place):
        pl.semaphore_signal(barrier, inc=1, device_id=device, device_id_type=MESH)

    peers("z", greet)
    peers("y", greet)
    peers("f", greet)

    mom_copy = pltpu.make_async_copy(mom_in, mom, local_sem.at[2])
    mas_copy = pltpu.make_async_copy(mas_in, mas, local_sem.at[3])
    lane = lax.broadcasted_iota(jnp.int32, (1, LANES), 1)
    own_copy.wait()
    value = own[...].astype(F32)
    squared = jnp.sum(jnp.sum(value * value, axis=0, keepdims=True), axis=1, keepdims=True)
    row = jnp.where(lane == rep, squared, 0.0)
    pl.semaphore_wait(barrier, nz + NY + nf - 3)

    def send_a(device, place):
        columns = pl.ds(pl.multiple_of(place * block, block), block)
        send(own.at[:, columns], ra.at[y], a_sem.at[0], a_sem.at[1], device)

    def exchange(axis, n, me, buffer, sems, row):
        buffer[me] = row
        peers(axis, lambda device, place: send(buffer.at[me], buffer.at[me], sems.at[0], sems.at[1], device))

        def total():
            drain(buffer.at[pl.ds(0, n - 1)], sems.at[1])
            return jnp.sum(buffer[...], axis=0)

        return total

    total = exchange("f", nf, f, fs, f_sem, row)
    peers("y", send_a)
    total = exchange("y", NY, y, ys, y_sem, total())
    mom_copy.start()
    mas_copy.start()

    block_copy.wait()
    drain(ra.at[pl.ds(0, NY - 1)], a_sem.at[1])
    for k in range(NY):
        arrived = ra[k].astype(F32)
        for j in range(tiles):
            rf[pl.ds(8 * (j * NY + k), rows), :] = arrived[:, j * LANES : (j + 1) * LANES]
    for r in range(rows):
        for j in range(tiles):
            column = pl.ds(j * LANES, LANES)
            tb[r, :, column] = rf[pl.ds(8 * j * NY + r, NY, stride=8), :].astype(BF16)

    def piece(place):
        columns = pl.ds(pl.multiple_of(lax.rem(place, halves) * chunk, chunk), chunk)
        return tb.at[lax.div(place, halves), :, columns]

    peers("z", lambda device, place: send(piece(place), zb.at[z], b_sem.at[0], b_sem.at[1], device))
    total = exchange("z", nz, z, zs, z_sem, total())
    zb[z] = piece(z)[...]

    row = total()
    drain(zb.at[pl.ds(0, nz - 1)], b_sem.at[1])
    held = zb[...].reshape(reps, chunk)

    def shares(squared):
        weight = jnp.where(lane < reps, 1.0 / jnp.sqrt(squared / entries + EPS), 0.0)
        return weight / jnp.sum(weight, axis=1, keepdims=True)

    def center_of(share):
        left = jnp.concatenate(split3(share), axis=0)[:, :reps]
        return jnp.sum(jnp.dot(left, held, preferred_element_type=F32), axis=0, keepdims=True)

    half = reps // 2
    spread = held.astype(F32) - center_of(shares(row))
    first, second = spread[:half], spread[half:]
    blank = jnp.zeros((LANES - reps, chunk), F32)

    def products(left, *right):
        return lax.dot_general(
            left, jnp.concatenate((*right, blank), axis=0), (((1,), (1,)), ((), ())),
            precision=lax.Precision.HIGHEST, preferred_element_type=F32,
        )

    at_row = lax.broadcasted_iota(jnp.int32, (half, LANES), 0)
    at_lane = lax.broadcasted_iota(jnp.int32, (half, LANES), 1)
    upper, lower = products(first, second, first), products(second, first, second)
    ends = jnp.sum(jnp.where(at_lane - half == at_row, lower, 0.0), axis=1, keepdims=True)
    kept = jnp.where((at_lane < half) | (at_lane - half >= at_row), upper, lower)
    kept = jnp.where(at_lane < reps, kept, jnp.where(at_lane == reps, ends, 0.0))

    share_rows = half // nf
    for g in range(nf):
        gm[g] = kept[g * share_rows : (g + 1) * share_rows]
    gx[f] = gm[f]
    peers("f", lambda device, place: send(gm.at[place], gx.at[f], gx_sem.at[0], gx_sem.at[1], device))
    drain(gx.at[pl.ds(0, nf - 1)], gx_sem.at[1])
    piece_sum = jnp.sum(gx[...], axis=0)
    piece_sum = exchange("y", NY, y, gy, gy_sem, piece_sum)()
    piece_sum = exchange("z", nz, z, gz, gz_sem, piece_sum)()
    gf[f] = piece_sum
    peers("f", lambda device, place: send(gf.at[f], gf.at[f], gf_sem.at[0], gf_sem.at[1], device))
    drain(gf.at[pl.ds(0, nf - 1)], gf_sem.at[1])
    for g in range(nf):
        gt[pl.ds(g * share_rows, share_rows), :] = gf[g]

    kept = gt[...]
    same = at_lane == at_row

    def to_row(column):
        return jnp.sum(jnp.where(same, column, 0.0), axis=0, keepdims=True)

    def to_column(line):
        return jnp.sum(jnp.where(same, line, 0.0), axis=1, keepdims=True)

    mixed = pltpu.roll(kept, LANES - half, 1)
    between = jnp.where(at_lane < half, kept, 0.0)
    upper = jnp.where((at_lane < half) & (at_lane >= at_row), mixed, 0.0)
    lower = jnp.where(at_lane < at_row, mixed, 0.0)
    ends_first = jnp.sum(jnp.where(same, mixed, 0.0), axis=0, keepdims=True)
    ends_second = to_row(kept[:, reps : reps + 1])
    squared = ends_first + pltpu.roll(ends_second, half, 1)
    share = shares(squared)
    share_first = jnp.where(lane < half, share, 0.0)
    share_second = jnp.where(lane < half, pltpu.roll(share, LANES - half, 1), 0.0)
    column_first, column_second = to_column(share_first), to_column(share_second)
    with_first = (
        jnp.sum(upper * column_first, axis=0, keepdims=True)
        + to_row(jnp.sum(upper * share_first + between * share_second, axis=1, keepdims=True))
        - ends_first * share_first
    )
    with_second = (
        jnp.sum(between * column_first + lower * column_second, axis=0, keepdims=True)
        + to_row(jnp.sum(lower * share_second, axis=1, keepdims=True))
        + ends_second * share_second
    )
    along = with_first + pltpu.roll(with_second, half, 1)
    squared = squared - 2.0 * along + jnp.sum(share * along, axis=1, keepdims=True)
    center = center_of(shares(jnp.maximum(squared, 0.0)))

    for part in range(parts):
        cd[y, z, pl.ds(part, 1), :] = center[:, part * LANES : (part + 1) * LANES]
    peers("z", lambda device, place: send(cd.at[y, z], cd.at[y, z], cz_send.at[0], cz_recv.at[z], device))

    def pass_on(i, carry):
        half = lax.div(i, 2) + lax.rem(i, 2)
        g = lax.rem(z + half * (1 - 2 * lax.rem(i, 2)) + nz, nz)

        @pl.when(i > 0)
        def _():
            drain(cd.at[0, g], cz_recv.at[g])

        peers("y", lambda device, place: send(cd.at[y, g], cd.at[y, g], cy_send.at[0], cy_recv.at[y], device))
        return carry

    lax.fori_loop(0, nz, pass_on, 0)
    mom_copy.wait()
    mas_copy.wait()

    def nearest(i):
        half = lax.div(i, 2) + lax.rem(i, 2)
        return lax.rem(y + half * (1 - 2 * lax.rem(i, 2)) + NY, NY)

    def out_copies(b):
        columns = pl.ds(pl.multiple_of(b * block, block), block)
        return [
            pltpu.make_async_copy(ref.at[:, columns], out.at[:, columns], out_sem.at[at, b])
            for at, (ref, out) in enumerate(((nm, nm_out), (ns, ns_out), (fw, fw_out)))
        ]

    def update(i, carry):
        b = nearest(i)

        @pl.when(i > 0)
        def _():
            drain(cd.at[b], cy_recv.at[b])

        for k in range(nz):
            cn[pl.ds(k * parts, parts), :] = cd[b, k]
        for j in range(tiles):
            here = pl.ds(pl.multiple_of(b * block + j * LANES, LANES), LANES)
            there = pl.ds(j, rows, stride=tiles)
            c = cn[there, :]
            momentum = 0.9 * mom[:, here] + c
            master = mas[:, here] - 0.7 * (c + 0.9 * momentum)
            nm[:, here] = momentum
            ns[:, here] = master
            nd[there, :] = master
        wb[f, b] = nd[...].astype(BF16)
        peers("x", lambda device, place: send(wb.at[f, b], wb.at[f, b], w_send.at[0], w_recv.at[b], device))
        send(wb.at[f, b], wb.at[f, b], v_send.at[0], v_recv.at[b], sibling)
        for copy in out_copies(b)[:2]:
            copy.start()
        return carry

    lax.fori_loop(0, NY, update, 0)

    def forward(i, carry):
        b = nearest(i)
        drain(wb.at[pl.ds(0, nf // 2 - 1), b], w_recv.at[b])

        def step(k, carry):
            g = 2 * lax.rem(x + 1 + k, nf // 2) + core
            send(wb.at[g, b], wb.at[g, b], v_send.at[0], v_recv.at[b], sibling)
            return carry

        return lax.fori_loop(0, nf // 2 - 1, step, carry)

    lax.fori_loop(0, NY, forward, 0)

    def place_weights(i, carry):
        b = nearest(i)
        drain(wb.at[pl.ds(0, nf // 2), b], v_recv.at[b])
        for g in range(nf):
            dense = wb[g, b].astype(F32)
            for r in range(rows):
                wf[pl.ds(g * rows + r, tiles, stride=nf * rows), :] = dense[r * tiles : (r + 1) * tiles]
        for j in range(tiles):
            here = pl.ds(pl.multiple_of(b * block + j * LANES, LANES), LANES)
            fw[:, here] = wf[pl.ds(j * nf * rows, nf * rows), :].astype(BF16)
        out_copies(b)[2].start()
        return carry

    lax.fori_loop(0, NY, place_weights, 0)

    def leave(i, carry):
        for copy in out_copies(i):
            copy.wait()
        return carry

    lax.fori_loop(0, NY, leave, 0)
    drain(ra.at[pl.ds(0, NY - 1)], a_sem.at[0])
    drain(zb.at[pl.ds(0, nz - 1)], b_sem.at[0])
    drain(fs.at[pl.ds(0, nf - 1)], f_sem.at[0])
    drain(ys.at[pl.ds(0, NY - 1)], y_sem.at[0])
    drain(zs.at[pl.ds(0, nz - 1)], z_sem.at[0])
    drain(gx.at[pl.ds(0, nf - 1)], gx_sem.at[0])
    drain(gy.at[pl.ds(0, NY - 1)], gy_sem.at[0])
    drain(gz.at[pl.ds(0, nz - 1)], gz_sem.at[0])
    drain(gf.at[pl.ds(0, nf - 1)], gf_sem.at[0])
    drain(cd.at[0, pl.ds(0, nz - 1)], cz_send.at[0])
    drain(cd.at[pl.ds(0, NY - 1)], cy_send.at[0])
    drain(wb.at[pl.ds(0, nf // 2 - 1)], w_send.at[0])
    drain(wb.at[pl.ds(0, nf // 2)], v_send.at[0])


def copy_kernel(count, *refs):
    sems = refs[-1]
    copies = [pltpu.make_async_copy(refs[i], refs[count + i], sems.at[i]) for i in range(count)]
    for copy in copies:
        copy.start()
    for copy in copies:
        copy.wait()


def solution(mesh):
    nf, nz = mesh.shape["fsdp"], mesh.shape["rep"] // NY

    def body(deltas, momentum, master):
        _, rows, width = deltas.shape
        block = width // NY
        chunk = block * rows // nz
        parts, tiles = chunk // LANES, block // LANES
        share_rows = NY * nz // 2 // nf
        anywhere = pl.BlockSpec(memory_space=pl.ANY)
        dma = pltpu.SemaphoreType.DMA
        outs = (
            jax.ShapeDtypeStruct((rows, width), F32),
            jax.ShapeDtypeStruct((rows, width), F32),
            jax.ShapeDtypeStruct((nf * rows, width), BF16),
        )
        results = pl.pallas_call(
            functools.partial(kernel, nf, nz),
            out_shape=outs,
            in_specs=[pl.BlockSpec(memory_space=pltpu.HBM)] * 3,
            out_specs=(anywhere,) * 3,
            scratch_shapes=[
                pltpu.VMEM((rows, width), BF16),
                pltpu.VMEM((rows, width), F32),
                pltpu.VMEM((rows, width), F32),
                pltpu.VMEM((rows, width), F32),
                pltpu.VMEM((rows, width), F32),
                pltpu.VMEM((nf * rows, width), BF16),
                pltpu.VMEM((NY, rows, block), BF16),
                pltpu.VMEM((tiles * NY * 8, LANES), F32),
                pltpu.VMEM((rows, NY, block), BF16),
                pltpu.VMEM((nz, NY, chunk), BF16),
                pltpu.VMEM((nf, 1, LANES), F32),
                pltpu.VMEM((NY, 1, LANES), F32),
                pltpu.VMEM((nz, 1, LANES), F32),
                pltpu.VMEM((nf, share_rows, LANES), F32),
                pltpu.VMEM((nf, share_rows, LANES), F32),
                pltpu.VMEM((NY, share_rows, LANES), F32),
                pltpu.VMEM((nz, share_rows, LANES), F32),
                pltpu.VMEM((nf, share_rows, LANES), F32),
                pltpu.VMEM((nf * share_rows, LANES), F32),
                pltpu.VMEM((NY, nz, parts, LANES), F32),
                pltpu.VMEM((rows * tiles, LANES), F32),
                pltpu.VMEM((rows * tiles, LANES), F32),
                pltpu.VMEM((nf, NY, rows * tiles, LANES), BF16),
                pltpu.VMEM((tiles * nf * rows, LANES), F32),
                dma((4,)),
                dma((3, NY)),
                dma((2,)),
                dma((2,)),
                dma((2,)),
                dma((2,)),
                dma((2,)),
                dma((2,)),
                dma((2,)),
                dma((2,)),
                dma((2,)),
                dma((1,)),
                dma((nz,)),
                dma((1,)),
                dma((NY,)),
                dma((1,)),
                dma((NY,)),
                dma((1,)),
                dma((NY,)),
            ],
            compiler_params=pltpu.CompilerParams(
                collective_id=0, has_side_effects=True, vmem_limit_bytes=16 * 2**20
            ),
        )(*(pltpu.with_memory_space_constraint(value, pltpu.HBM) for value in (deltas, momentum, master)))
        return pl.pallas_call(
            functools.partial(copy_kernel, len(outs)),
            out_shape=outs,
            in_specs=[pl.BlockSpec(memory_space=pltpu.VMEM)] * len(outs),
            out_specs=(anywhere,) * len(outs),
            scratch_shapes=[dma((len(outs),))],
            compiler_params=pltpu.CompilerParams(vmem_limit_bytes=16 * 2**20),
        )(*results)

    placed = (P("rep", "fsdp", None), P("fsdp", None), P("fsdp", None))
    return jax.shard_map(
        body,
        mesh=mesh,
        in_specs=placed,
        out_specs=(P("fsdp", None), P("fsdp", None), P()),
        check_vma=False,
    )
```

```python
import functools

import jax
import jax.numpy as jnp
from jax import lax
from jax.experimental import pallas as pl
from jax.experimental.pallas import tpu as pltpu
from jax.sharding import PartitionSpec as P

EPS = 1e-06
NY = 8
LANES = 128
MESH = pl.DeviceIdType.MESH
F32, BF16 = jnp.float32, jnp.bfloat16


def split3(value):
    high = value.astype(BF16)
    rest = value - high.astype(F32)
    mid = rest.astype(BF16)
    low = (rest - mid.astype(F32)).astype(BF16)
    return high, mid, low


def kernel(
    nf, nz, delta, mom_in, mas_in, nm_out, ns_out, fw_out,
    own, mom, mas, nm, ns, fw, ra, rf, tb, zb, fs, ys, zs, gm, gx, gy, gz, gf, gt, cd, cn, nd, wb, wf,
    z_answer, local_sem, out_sem, a_sem, b_sem, f_sem, y_sem, z_sem, gx_sem, gy_sem, gz_sem, gf_sem, cz_send, cz_recv, cy_send, cy_recv, w_send, w_recv, v_send, v_recv,
):
    rows, width = own.shape
    block = width // NY
    halves = nz // rows
    chunk = block // halves
    tiles = block // LANES
    parts = chunk // LANES
    reps = NY * nz
    entries = nf * rows * width

    rep, f = lax.axis_index("rep"), lax.axis_index("fsdp")
    y, z = lax.rem(rep, NY), lax.div(rep, NY)

    x, core = lax.div(f, 2), lax.rem(f, 2)
    sibling = (rep, f + 1 - 2 * core)

    def peers(axis, visit):
        n = {"x": nf // 2, "f": nf, "y": NY, "z": nz}[axis]
        me = {"x": x, "f": f, "y": y, "z": z}[axis]

        def step(i, carry):
            half = lax.div(i + 1, 2)
            place = lax.rem(me + n // 2 + half * (2 * lax.rem(i, 2) - 1) + n, n)
            if axis == "x":
                device = (rep, 2 * place + core)
            elif axis == "f":
                device = (rep, place)
            elif axis == "y":
                device = (z * NY + place, f)
            else:
                device = (place * NY + y, f)
            visit(device, place)
            return carry

        lax.fori_loop(0, n - 1, step, 0)

    def send(src, dst, send_sem, recv_sem, device):
        pltpu.make_async_remote_copy(
            src_ref=src, dst_ref=dst, send_sem=send_sem, recv_sem=recv_sem,
            device_id=device, device_id_type=MESH,
        ).start()

    def drain(ref, sem):
        pltpu.make_async_copy(ref, ref, sem).wait()

    own_copy = pltpu.make_async_copy(delta.at[0], own, local_sem.at[0])
    own_copy.start()
    mine = pl.ds(pl.multiple_of(y * block, block), block)
    block_copy = pltpu.make_async_copy(delta.at[0, :, mine], ra.at[y], local_sem.at[1])
    block_copy.start()

    barrier = pltpu.get_barrier_semaphore()

    def above(visit):
        def check(device, place):
            @pl.when(place > z)
            def _():
                visit(device, place)

        peers("z", check)

    def below(visit):
        def check(device, place):
            @pl.when(place < z)
            def _():
                visit(device, place)

        peers("z", check)

    def tell(sem):
        return lambda device, place: pl.semaphore_signal(sem, inc=1, device_id=device, device_id_type=MESH)

    peers("y", tell(barrier))
    above(tell(barrier))
    peers("f", tell(barrier))

    mom_copy = pltpu.make_async_copy(mom_in, mom, local_sem.at[2])
    mas_copy = pltpu.make_async_copy(mas_in, mas, local_sem.at[3])
    lane = lax.broadcasted_iota(jnp.int32, (1, LANES), 1)
    own_copy.wait()
    value = own[...].astype(F32)
    squared = jnp.sum(jnp.sum(value * value, axis=0, keepdims=True), axis=1, keepdims=True)
    row = jnp.where(lane == rep, squared, 0.0)
    pl.semaphore_wait(barrier, NY + nf - 2 + z)
    below(tell(z_answer))

    def send_a(device, place):
        columns = pl.ds(pl.multiple_of(place * block, block), block)
        send(own.at[:, columns], ra.at[y], a_sem.at[0], a_sem.at[1], device)

    def exchange(axis, n, me, buffer, sems, row):
        buffer[me] = row
        peers(axis, lambda device, place: send(buffer.at[me], buffer.at[me], sems.at[0], sems.at[1], device))

        def total():
            drain(buffer.at[pl.ds(0, n - 1)], sems.at[1])
            return jnp.sum(buffer[...], axis=0)

        return total

    peers("y", send_a)
    total = exchange("f", nf, f, fs, f_sem, row)
    total = exchange("y", NY, y, ys, y_sem, total())
    mom_copy.start()
    mas_copy.start()

    block_copy.wait()
    drain(ra.at[pl.ds(0, NY - 1)], a_sem.at[1])
    for k in range(NY):
        arrived = ra[k].astype(F32)
        for j in range(tiles):
            rf[pl.ds(8 * (j * NY + k), rows), :] = arrived[:, j * LANES : (j + 1) * LANES]
    for r in range(rows):
        for j in range(tiles):
            column = pl.ds(j * LANES, LANES)
            tb[r, :, column] = rf[pl.ds(8 * j * NY + r, NY, stride=8), :].astype(BF16)

    def piece(place):
        columns = pl.ds(pl.multiple_of(lax.rem(place, halves) * chunk, chunk), chunk)
        return tb.at[lax.div(place, halves), :, columns]

    def send_b(device, place):
        send(piece(place), zb.at[z], b_sem.at[0], b_sem.at[1], device)

    below(send_b)

    @pl.when(z < nz - 1)
    def _():
        pl.semaphore_wait(z_answer, nz - 1 - z)

    above(send_b)
    total = exchange("z", nz, z, zs, z_sem, total())
    zb[z] = piece(z)[...]

    row = total()
    drain(zb.at[pl.ds(0, nz - 1)], b_sem.at[1])
    held = zb[...].reshape(reps, chunk)

    def shares(squared):
        weight = jnp.where(lane < reps, 1.0 / jnp.sqrt(squared / entries + EPS), 0.0)
        return weight / jnp.sum(weight, axis=1, keepdims=True)

    def center_of(share):
        left = jnp.concatenate(split3(share), axis=0)[:, :reps]
        return jnp.sum(jnp.dot(left, held, preferred_element_type=F32), axis=0, keepdims=True)

    half = reps // 2
    spread = held.astype(F32) - center_of(shares(row))
    first, second = spread[:half], spread[half:]
    blank = jnp.zeros((LANES - reps, chunk), F32)

    def products(left, *right):
        return lax.dot_general(
            left, jnp.concatenate((*right, blank), axis=0), (((1,), (1,)), ((), ())),
            precision=lax.Precision.HIGHEST, preferred_element_type=F32,
        )

    at_row = lax.broadcasted_iota(jnp.int32, (half, LANES), 0)
    at_lane = lax.broadcasted_iota(jnp.int32, (half, LANES), 1)
    upper, lower = products(first, second, first), products(second, first, second)
    ends = jnp.sum(jnp.where(at_lane - half == at_row, lower, 0.0), axis=1, keepdims=True)
    kept = jnp.where((at_lane < half) | (at_lane - half >= at_row), upper, lower)
    kept = jnp.where(at_lane < reps, kept, jnp.where(at_lane == reps, ends, 0.0))

    share_rows = half // nf
    for g in range(nf):
        gm[g] = kept[g * share_rows : (g + 1) * share_rows]
    gx[f] = gm[f]
    peers("f", lambda device, place: send(gm.at[place], gx.at[f], gx_sem.at[0], gx_sem.at[1], device))
    drain(gx.at[pl.ds(0, nf - 1)], gx_sem.at[1])
    piece_sum = jnp.sum(gx[...], axis=0)
    piece_sum = exchange("y", NY, y, gy, gy_sem, piece_sum)()
    piece_sum = exchange("z", nz, z, gz, gz_sem, piece_sum)()
    gf[f] = piece_sum
    peers("f", lambda device, place: send(gf.at[f], gf.at[f], gf_sem.at[0], gf_sem.at[1], device))
    drain(gf.at[pl.ds(0, nf - 1)], gf_sem.at[1])
    for g in range(nf):
        gt[pl.ds(g * share_rows, share_rows), :] = gf[g]

    kept = gt[...]
    same = at_lane == at_row

    def to_row(column):
        return jnp.sum(jnp.where(same, column, 0.0), axis=0, keepdims=True)

    def to_column(line):
        return jnp.sum(jnp.where(same, line, 0.0), axis=1, keepdims=True)

    mixed = pltpu.roll(kept, LANES - half, 1)
    between = jnp.where(at_lane < half, kept, 0.0)
    upper = jnp.where((at_lane < half) & (at_lane >= at_row), mixed, 0.0)
    lower = jnp.where(at_lane < at_row, mixed, 0.0)
    ends_first = jnp.sum(jnp.where(same, mixed, 0.0), axis=0, keepdims=True)
    ends_second = to_row(kept[:, reps : reps + 1])
    squared = ends_first + pltpu.roll(ends_second, half, 1)
    share = shares(squared)
    share_first = jnp.where(lane < half, share, 0.0)
    share_second = jnp.where(lane < half, pltpu.roll(share, LANES - half, 1), 0.0)
    column_first, column_second = to_column(share_first), to_column(share_second)
    with_first = (
        jnp.sum(upper * column_first, axis=0, keepdims=True)
        + to_row(jnp.sum(upper * share_first + between * share_second, axis=1, keepdims=True))
        - ends_first * share_first
    )
    with_second = (
        jnp.sum(between * column_first + lower * column_second, axis=0, keepdims=True)
        + to_row(jnp.sum(lower * share_second, axis=1, keepdims=True))
        + ends_second * share_second
    )
    along = with_first + pltpu.roll(with_second, half, 1)
    squared = squared - 2.0 * along + jnp.sum(share * along, axis=1, keepdims=True)
    center = center_of(shares(jnp.maximum(squared, 0.0)))

    for part in range(parts):
        cd[y, z, pl.ds(part, 1), :] = center[:, part * LANES : (part + 1) * LANES]
    peers("z", lambda device, place: send(cd.at[y, z], cd.at[y, z], cz_send.at[0], cz_recv.at[z], device))

    def pass_on(i, carry):
        half = lax.div(i, 2) + lax.rem(i, 2)
        g = lax.rem(z + half * (1 - 2 * lax.rem(i, 2)) + nz, nz)

        @pl.when(i > 0)
        def _():
            drain(cd.at[0, g], cz_recv.at[g])

        peers("y", lambda device, place: send(cd.at[y, g], cd.at[y, g], cy_send.at[0], cy_recv.at[y], device))
        return carry

    lax.fori_loop(0, nz, pass_on, 0)
    mom_copy.wait()
    mas_copy.wait()

    def nearest(i):
        half = lax.div(i, 2) + lax.rem(i, 2)
        return lax.rem(y + half * (1 - 2 * lax.rem(i, 2)) + NY, NY)

    def out_copies(b):
        columns = pl.ds(pl.multiple_of(b * block, block), block)
        return [
            pltpu.make_async_copy(ref.at[:, columns], out.at[:, columns], out_sem.at[at, b])
            for at, (ref, out) in enumerate(((nm, nm_out), (ns, ns_out), (fw, fw_out)))
        ]

    def update(i, carry):
        b = nearest(i)

        @pl.when(i > 0)
        def _():
            drain(cd.at[b], cy_recv.at[b])

        for k in range(nz):
            cn[pl.ds(k * parts, parts), :] = cd[b, k]
        for j in range(tiles):
            here = pl.ds(pl.multiple_of(b * block + j * LANES, LANES), LANES)
            there = pl.ds(j, rows, stride=tiles)
            c = cn[there, :]
            momentum = 0.9 * mom[:, here] + c
            master = mas[:, here] - 0.7 * (c + 0.9 * momentum)
            nm[:, here] = momentum
            ns[:, here] = master
            nd[there, :] = master
        wb[f, b] = nd[...].astype(BF16)
        peers("x", lambda device, place: send(wb.at[f, b], wb.at[f, b], w_send.at[0], w_recv.at[b], device))
        send(wb.at[f, b], wb.at[f, b], v_send.at[0], v_recv.at[b], sibling)
        for copy in out_copies(b)[:2]:
            copy.start()
        return carry

    lax.fori_loop(0, NY, update, 0)

    def forward(i, carry):
        b = nearest(i)
        drain(wb.at[pl.ds(0, nf // 2 - 1), b], w_recv.at[b])

        def step(k, carry):
            g = 2 * lax.rem(x + 1 + k, nf // 2) + core
            send(wb.at[g, b], wb.at[g, b], v_send.at[0], v_recv.at[b], sibling)
            return carry

        return lax.fori_loop(0, nf // 2 - 1, step, carry)

    lax.fori_loop(0, NY, forward, 0)

    def place_weights(i, carry):
        b = nearest(i)
        drain(wb.at[pl.ds(0, nf // 2), b], v_recv.at[b])
        for g in range(nf):
            dense = wb[g, b].astype(F32)
            for r in range(rows):
                wf[pl.ds(g * rows + r, tiles, stride=nf * rows), :] = dense[r * tiles : (r + 1) * tiles]
        for j in range(tiles):
            here = pl.ds(pl.multiple_of(b * block + j * LANES, LANES), LANES)
            fw[:, here] = wf[pl.ds(j * nf * rows, nf * rows), :].astype(BF16)
        out_copies(b)[2].start()
        return carry

    lax.fori_loop(0, NY, place_weights, 0)

    def leave(i, carry):
        for copy in out_copies(i):
            copy.wait()
        return carry

    lax.fori_loop(0, NY, leave, 0)
    drain(ra.at[pl.ds(0, NY - 1)], a_sem.at[0])
    drain(zb.at[pl.ds(0, nz - 1)], b_sem.at[0])
    drain(fs.at[pl.ds(0, nf - 1)], f_sem.at[0])
    drain(ys.at[pl.ds(0, NY - 1)], y_sem.at[0])
    drain(zs.at[pl.ds(0, nz - 1)], z_sem.at[0])
    drain(gx.at[pl.ds(0, nf - 1)], gx_sem.at[0])
    drain(gy.at[pl.ds(0, NY - 1)], gy_sem.at[0])
    drain(gz.at[pl.ds(0, nz - 1)], gz_sem.at[0])
    drain(gf.at[pl.ds(0, nf - 1)], gf_sem.at[0])
    drain(cd.at[0, pl.ds(0, nz - 1)], cz_send.at[0])
    drain(cd.at[pl.ds(0, NY - 1)], cy_send.at[0])
    drain(wb.at[pl.ds(0, nf // 2 - 1)], w_send.at[0])
    drain(wb.at[pl.ds(0, nf // 2)], v_send.at[0])


def copy_kernel(count, *refs):
    sems = refs[-1]
    copies = [pltpu.make_async_copy(refs[i], refs[count + i], sems.at[i]) for i in range(count)]
    for copy in copies:
        copy.start()
    for copy in copies:
        copy.wait()


def solution(mesh):
    nf, nz = mesh.shape["fsdp"], mesh.shape["rep"] // NY

    def body(deltas, momentum, master):
        _, rows, width = deltas.shape
        block = width // NY
        chunk = block * rows // nz
        parts, tiles = chunk // LANES, block // LANES
        share_rows = NY * nz // 2 // nf
        anywhere = pl.BlockSpec(memory_space=pl.ANY)
        dma = pltpu.SemaphoreType.DMA
        outs = (
            jax.ShapeDtypeStruct((rows, width), F32),
            jax.ShapeDtypeStruct((rows, width), F32),
            jax.ShapeDtypeStruct((nf * rows, width), BF16),
        )
        results = pl.pallas_call(
            functools.partial(kernel, nf, nz),
            out_shape=outs,
            in_specs=[pl.BlockSpec(memory_space=pltpu.HBM)] * 3,
            out_specs=(anywhere,) * 3,
            scratch_shapes=[
                pltpu.VMEM((rows, width), BF16),
                pltpu.VMEM((rows, width), F32),
                pltpu.VMEM((rows, width), F32),
                pltpu.VMEM((rows, width), F32),
                pltpu.VMEM((rows, width), F32),
                pltpu.VMEM((nf * rows, width), BF16),
                pltpu.VMEM((NY, rows, block), BF16),
                pltpu.VMEM((tiles * NY * 8, LANES), F32),
                pltpu.VMEM((rows, NY, block), BF16),
                pltpu.VMEM((nz, NY, chunk), BF16),
                pltpu.VMEM((nf, 1, LANES), F32),
                pltpu.VMEM((NY, 1, LANES), F32),
                pltpu.VMEM((nz, 1, LANES), F32),
                pltpu.VMEM((nf, share_rows, LANES), F32),
                pltpu.VMEM((nf, share_rows, LANES), F32),
                pltpu.VMEM((NY, share_rows, LANES), F32),
                pltpu.VMEM((nz, share_rows, LANES), F32),
                pltpu.VMEM((nf, share_rows, LANES), F32),
                pltpu.VMEM((nf * share_rows, LANES), F32),
                pltpu.VMEM((NY, nz, parts, LANES), F32),
                pltpu.VMEM((rows * tiles, LANES), F32),
                pltpu.VMEM((rows * tiles, LANES), F32),
                pltpu.VMEM((nf, NY, rows * tiles, LANES), BF16),
                pltpu.VMEM((tiles * nf * rows, LANES), F32),
                pltpu.SemaphoreType.REGULAR,
                dma((4,)),
                dma((3, NY)),
                dma((2,)),
                dma((2,)),
                dma((2,)),
                dma((2,)),
                dma((2,)),
                dma((2,)),
                dma((2,)),
                dma((2,)),
                dma((2,)),
                dma((1,)),
                dma((nz,)),
                dma((1,)),
                dma((NY,)),
                dma((1,)),
                dma((NY,)),
                dma((1,)),
                dma((NY,)),
            ],
            compiler_params=pltpu.CompilerParams(
                collective_id=0, has_side_effects=True, vmem_limit_bytes=16 * 2**20
            ),
        )(*(pltpu.with_memory_space_constraint(value, pltpu.HBM) for value in (deltas, momentum, master)))
        return pl.pallas_call(
            functools.partial(copy_kernel, len(outs)),
            out_shape=outs,
            in_specs=[pl.BlockSpec(memory_space=pltpu.VMEM)] * len(outs),
            out_specs=(anywhere,) * len(outs),
            scratch_shapes=[dma((len(outs),))],
            compiler_params=pltpu.CompilerParams(vmem_limit_bytes=16 * 2**20),
        )(*results)

    placed = (P("rep", "fsdp", None), P("fsdp", None), P("fsdp", None))
    return jax.shard_map(
        body,
        mesh=mesh,
        in_specs=placed,
        out_specs=(P("fsdp", None), P("fsdp", None), P()),
        check_vma=False,
    )
```

```python
import functools

import jax
import jax.numpy as jnp
from jax import lax
from jax.experimental import pallas as pl
from jax.experimental.pallas import tpu as pltpu
from jax.sharding import PartitionSpec as P

EPS = 1e-06
NY = 8
LANES = 128
MESH = pl.DeviceIdType.MESH
F32, BF16 = jnp.float32, jnp.bfloat16


def split3(value):
    high = value.astype(BF16)
    rest = value - high.astype(F32)
    mid = rest.astype(BF16)
    low = (rest - mid.astype(F32)).astype(BF16)
    return high, mid, low


def kernel(
    nf, nz, delta, mom_in, mas_in, nm_out, ns_out, fw_out,
    own, mom, mas, nm, ns, ra, rf, tb, zb, fs, ys, zs, gm, gx, gy, gz, gf, gt, cd, cn, nd, wb, wf,
    z_answer, local_sem, out_sem, a_sem, b_sem, f_sem, y_sem, z_sem, gx_sem, gy_sem, gz_sem, gf_sem, cz_send, cz_recv, cy_send, cy_recv, w_send, w_recv, v_send, v_recv,
):
    rows, width = own.shape
    block = width // NY
    halves = nz // rows
    chunk = block // halves
    tiles = block // LANES
    parts = chunk // LANES
    reps = NY * nz
    entries = nf * rows * width

    rep, f = lax.axis_index("rep"), lax.axis_index("fsdp")
    y, z = lax.rem(rep, NY), lax.div(rep, NY)

    x, core = lax.div(f, 2), lax.rem(f, 2)
    sibling = (rep, f + 1 - 2 * core)

    def peers(axis, visit):
        n = {"x": nf // 2, "f": nf, "y": NY, "z": nz}[axis]
        me = {"x": x, "f": f, "y": y, "z": z}[axis]

        def step(i, carry):
            half = lax.div(i + 1, 2)
            place = lax.rem(me + n // 2 + half * (2 * lax.rem(i, 2) - 1) + n, n)
            if axis == "x":
                device = (rep, 2 * place + core)
            elif axis == "f":
                device = (rep, place)
            elif axis == "y":
                device = (z * NY + place, f)
            else:
                device = (place * NY + y, f)
            visit(device, place)
            return carry

        lax.fori_loop(0, n - 1, step, 0)

    def send(src, dst, send_sem, recv_sem, device):
        pltpu.make_async_remote_copy(
            src_ref=src, dst_ref=dst, send_sem=send_sem, recv_sem=recv_sem,
            device_id=device, device_id_type=MESH,
        ).start()

    def drain(ref, sem):
        pltpu.make_async_copy(ref, ref, sem).wait()

    own_copy = pltpu.make_async_copy(delta.at[0], own, local_sem.at[0])
    own_copy.start()
    mine = pl.ds(pl.multiple_of(y * block, block), block)
    block_copy = pltpu.make_async_copy(delta.at[0, :, mine], ra.at[y], local_sem.at[1])
    block_copy.start()

    barrier = pltpu.get_barrier_semaphore()

    def above(visit):
        def check(device, place):
            @pl.when(place > z)
            def _():
                visit(device, place)

        peers("z", check)

    def below(visit):
        def check(device, place):
            @pl.when(place < z)
            def _():
                visit(device, place)

        peers("z", check)

    def tell(sem):
        return lambda device, place: pl.semaphore_signal(sem, inc=1, device_id=device, device_id_type=MESH)

    peers("y", tell(barrier))
    above(tell(barrier))
    peers("f", tell(barrier))

    mom_copy = pltpu.make_async_copy(mom_in, mom, local_sem.at[2])
    mas_copy = pltpu.make_async_copy(mas_in, mas, local_sem.at[3])
    lane = lax.broadcasted_iota(jnp.int32, (1, LANES), 1)
    own_copy.wait()
    value = own[...].astype(F32)
    squared = jnp.sum(jnp.sum(value * value, axis=0, keepdims=True), axis=1, keepdims=True)
    row = jnp.where(lane == rep, squared, 0.0)
    pl.semaphore_wait(barrier, NY + nf - 2 + z)
    below(tell(z_answer))

    def send_a(device, place):
        columns = pl.ds(pl.multiple_of(place * block, block), block)
        send(own.at[:, columns], ra.at[y], a_sem.at[0], a_sem.at[1], device)

    def exchange(axis, n, me, buffer, sems, row):
        buffer[me] = row
        peers(axis, lambda device, place: send(buffer.at[me], buffer.at[me], sems.at[0], sems.at[1], device))

        def total():
            drain(buffer.at[pl.ds(0, n - 1)], sems.at[1])
            return jnp.sum(buffer[...], axis=0)

        return total

    peers("y", send_a)
    total = exchange("f", nf, f, fs, f_sem, row)
    total = exchange("y", NY, y, ys, y_sem, total())
    mom_copy.start()
    mas_copy.start()

    block_copy.wait()
    drain(ra.at[pl.ds(0, NY - 1)], a_sem.at[1])
    for k in range(NY):
        arrived = ra[k].astype(F32)
        for j in range(tiles):
            rf[pl.ds(8 * (j * NY + k), rows), :] = arrived[:, j * LANES : (j + 1) * LANES]

    def piece(place):
        columns = pl.ds(pl.multiple_of(lax.rem(place, halves) * chunk, chunk), chunk)
        return tb.at[lax.div(place, halves), :, columns]

    def send_b(device, place):
        send(piece(place), zb.at[z], b_sem.at[0], b_sem.at[1], device)

    for r in range(rows):
        for j in range(tiles):
            column = pl.ds(j * LANES, LANES)
            tb[r, :, column] = rf[pl.ds(8 * j * NY + r, NY, stride=8), :].astype(BF16)
        for place in range(r * halves, (r + 1) * halves):

            @pl.when(place < z)
            def _():
                send_b((place * NY + y, f), place)

    @pl.when(z < nz - 1)
    def _():
        pl.semaphore_wait(z_answer, nz - 1 - z)

    above(send_b)
    total = exchange("z", nz, z, zs, z_sem, total())
    zb[z] = piece(z)[...]

    row = total()
    drain(zb.at[pl.ds(0, nz - 1)], b_sem.at[1])
    held = zb[...].reshape(reps, chunk)

    def shares(squared):
        weight = jnp.where(lane < reps, 1.0 / jnp.sqrt(squared / entries + EPS), 0.0)
        return weight / jnp.sum(weight, axis=1, keepdims=True)

    def center_of(share):
        left = jnp.concatenate(split3(share), axis=0)[:, :reps]
        return jnp.sum(jnp.dot(left, held, preferred_element_type=F32), axis=0, keepdims=True)

    half = reps // 2
    spread = held.astype(F32) - center_of(shares(row))
    first, second = spread[:half], spread[half:]
    blank = jnp.zeros((LANES - reps, chunk), F32)

    def products(left, *right):
        return lax.dot_general(
            left, jnp.concatenate((*right, blank), axis=0), (((1,), (1,)), ((), ())),
            precision=lax.Precision.HIGHEST, preferred_element_type=F32,
        )

    at_row = lax.broadcasted_iota(jnp.int32, (half, LANES), 0)
    at_lane = lax.broadcasted_iota(jnp.int32, (half, LANES), 1)
    upper, lower = products(first, second, first), products(second, first, second)
    ends = jnp.sum(jnp.where(at_lane - half == at_row, lower, 0.0), axis=1, keepdims=True)
    kept = jnp.where((at_lane < half) | (at_lane - half >= at_row), upper, lower)
    kept = jnp.where(at_lane < reps, kept, jnp.where(at_lane == reps, ends, 0.0))

    share_rows = half // nf
    for g in range(nf):
        gm[g] = kept[g * share_rows : (g + 1) * share_rows]
    gx[f] = gm[f]
    peers("f", lambda device, place: send(gm.at[place], gx.at[f], gx_sem.at[0], gx_sem.at[1], device))
    drain(gx.at[pl.ds(0, nf - 1)], gx_sem.at[1])
    piece_sum = jnp.sum(gx[...], axis=0)
    piece_sum = exchange("y", NY, y, gy, gy_sem, piece_sum)()
    piece_sum = exchange("z", nz, z, gz, gz_sem, piece_sum)()
    gf[f] = piece_sum
    peers("f", lambda device, place: send(gf.at[f], gf.at[f], gf_sem.at[0], gf_sem.at[1], device))
    drain(gf.at[pl.ds(0, nf - 1)], gf_sem.at[1])
    for g in range(nf):
        gt[pl.ds(g * share_rows, share_rows), :] = gf[g]

    kept = gt[...]
    same = at_lane == at_row

    def to_row(column):
        return jnp.sum(jnp.where(same, column, 0.0), axis=0, keepdims=True)

    def to_column(line):
        return jnp.sum(jnp.where(same, line, 0.0), axis=1, keepdims=True)

    mixed = pltpu.roll(kept, LANES - half, 1)
    between = jnp.where(at_lane < half, kept, 0.0)
    upper = jnp.where((at_lane < half) & (at_lane >= at_row), mixed, 0.0)
    lower = jnp.where(at_lane < at_row, mixed, 0.0)
    ends_first = jnp.sum(jnp.where(same, mixed, 0.0), axis=0, keepdims=True)
    ends_second = to_row(kept[:, reps : reps + 1])
    squared = ends_first + pltpu.roll(ends_second, half, 1)
    share = shares(squared)
    share_first = jnp.where(lane < half, share, 0.0)
    share_second = jnp.where(lane < half, pltpu.roll(share, LANES - half, 1), 0.0)
    column_first, column_second = to_column(share_first), to_column(share_second)
    with_first = (
        jnp.sum(upper * column_first, axis=0, keepdims=True)
        + to_row(jnp.sum(upper * share_first + between * share_second, axis=1, keepdims=True))
        - ends_first * share_first
    )
    with_second = (
        jnp.sum(between * column_first + lower * column_second, axis=0, keepdims=True)
        + to_row(jnp.sum(lower * share_second, axis=1, keepdims=True))
        + ends_second * share_second
    )
    along = with_first + pltpu.roll(with_second, half, 1)
    squared = squared - 2.0 * along + jnp.sum(share * along, axis=1, keepdims=True)
    center = center_of(shares(jnp.maximum(squared, 0.0)))

    for part in range(parts):
        cd[y, z, pl.ds(part, 1), :] = center[:, part * LANES : (part + 1) * LANES]
    peers("z", lambda device, place: send(cd.at[y, z], cd.at[y, z], cz_send.at[0], cz_recv.at[z], device))

    def pass_on(i, carry):
        half = lax.div(i, 2) + lax.rem(i, 2)
        g = lax.rem(z + half * (1 - 2 * lax.rem(i, 2)) + nz, nz)

        @pl.when(i > 0)
        def _():
            drain(cd.at[0, g], cz_recv.at[g])

        peers("y", lambda device, place: send(cd.at[y, g], cd.at[y, g], cy_send.at[0], cy_recv.at[y], device))
        return carry

    lax.fori_loop(0, nz, pass_on, 0)
    mom_copy.wait()
    mas_copy.wait()

    def nearest(i):
        half = lax.div(i, 2) + lax.rem(i, 2)
        return lax.rem(y + half * (1 - 2 * lax.rem(i, 2)) + NY, NY)

    def out_copies(b):
        columns = pl.ds(pl.multiple_of(b * block, block), block)
        return [
            pltpu.make_async_copy(ref.at[:, columns], out.at[:, columns], out_sem.at[at, b])
            for at, (ref, out) in enumerate(((nm, nm_out), (ns, ns_out)))
        ]

    def update(i, carry):
        b = nearest(i)

        @pl.when(i > 0)
        def _():
            drain(cd.at[b], cy_recv.at[b])

        for k in range(nz):
            cn[pl.ds(k * parts, parts), :] = cd[b, k]
        for j in range(tiles):
            here = pl.ds(pl.multiple_of(b * block + j * LANES, LANES), LANES)
            there = pl.ds(j, rows, stride=tiles)
            c = cn[there, :]
            momentum = 0.9 * mom[:, here] + c
            master = mas[:, here] - 0.7 * (c + 0.9 * momentum)
            nm[:, here] = momentum
            ns[:, here] = master
            nd[there, :] = master
        wb[f, b] = nd[...].astype(BF16)
        peers("x", lambda device, place: send(wb.at[f, b], wb.at[f, b], w_send.at[0], w_recv.at[b], device))
        send(wb.at[f, b], wb.at[f, b], v_send.at[0], v_recv.at[b], sibling)
        for copy in out_copies(b):
            copy.start()
        return carry

    lax.fori_loop(0, NY, update, 0)

    def forward(i, carry):
        b = nearest(i)
        drain(wb.at[pl.ds(0, nf // 2 - 1), b], w_recv.at[b])

        def step(k, carry):
            g = 2 * lax.rem(x + 1 + k, nf // 2) + core
            send(wb.at[g, b], wb.at[g, b], v_send.at[0], v_recv.at[b], sibling)
            return carry

        return lax.fori_loop(0, nf // 2 - 1, step, carry)

    lax.fori_loop(0, NY, forward, 0)

    def place_weights(i, carry):
        b = nearest(i)
        drain(wb.at[pl.ds(0, nf // 2), b], v_recv.at[b])
        for g in range(nf):
            dense = wb[g, b].astype(F32)
            for r in range(rows):
                wf[pl.ds(g * rows + r, tiles, stride=nf * rows), :] = dense[r * tiles : (r + 1) * tiles]
        for j in range(tiles):
            here = pl.ds(pl.multiple_of(b * block + j * LANES, LANES), LANES)
            fw_out[:, here] = wf[pl.ds(j * nf * rows, nf * rows), :].astype(BF16)
        return carry

    lax.fori_loop(0, NY, place_weights, 0)

    def leave(i, carry):
        for copy in out_copies(i):
            copy.wait()
        return carry

    lax.fori_loop(0, NY, leave, 0)
    drain(ra.at[pl.ds(0, NY - 1)], a_sem.at[0])
    drain(zb.at[pl.ds(0, nz - 1)], b_sem.at[0])
    drain(fs.at[pl.ds(0, nf - 1)], f_sem.at[0])
    drain(ys.at[pl.ds(0, NY - 1)], y_sem.at[0])
    drain(zs.at[pl.ds(0, nz - 1)], z_sem.at[0])
    drain(gx.at[pl.ds(0, nf - 1)], gx_sem.at[0])
    drain(gy.at[pl.ds(0, NY - 1)], gy_sem.at[0])
    drain(gz.at[pl.ds(0, nz - 1)], gz_sem.at[0])
    drain(gf.at[pl.ds(0, nf - 1)], gf_sem.at[0])
    drain(cd.at[0, pl.ds(0, nz - 1)], cz_send.at[0])
    drain(cd.at[pl.ds(0, NY - 1)], cy_send.at[0])
    drain(wb.at[pl.ds(0, nf // 2 - 1)], w_send.at[0])
    drain(wb.at[pl.ds(0, nf // 2)], v_send.at[0])


def copy_kernel(count, *refs):
    sems = refs[-1]
    copies = [pltpu.make_async_copy(refs[i], refs[count + i], sems.at[i]) for i in range(count)]
    for copy in copies:
        copy.start()
    for copy in copies:
        copy.wait()


def solution(mesh):
    nf, nz = mesh.shape["fsdp"], mesh.shape["rep"] // NY

    def body(deltas, momentum, master):
        _, rows, width = deltas.shape
        block = width // NY
        chunk = block * rows // nz
        parts, tiles = chunk // LANES, block // LANES
        share_rows = NY * nz // 2 // nf
        anywhere = pl.BlockSpec(memory_space=pl.ANY)
        dma = pltpu.SemaphoreType.DMA
        outs = (
            jax.ShapeDtypeStruct((rows, width), F32),
            jax.ShapeDtypeStruct((rows, width), F32),
            jax.ShapeDtypeStruct((nf * rows, width), BF16),
        )
        results = pl.pallas_call(
            functools.partial(kernel, nf, nz),
            out_shape=outs,
            in_specs=[pl.BlockSpec(memory_space=pltpu.HBM)] * 3,
            out_specs=(anywhere, anywhere, pl.BlockSpec(memory_space=pltpu.VMEM)),
            scratch_shapes=[
                pltpu.VMEM((rows, width), BF16),
                pltpu.VMEM((rows, width), F32),
                pltpu.VMEM((rows, width), F32),
                pltpu.VMEM((rows, width), F32),
                pltpu.VMEM((rows, width), F32),
                pltpu.VMEM((NY, rows, block), BF16),
                pltpu.VMEM((tiles * NY * 8, LANES), F32),
                pltpu.VMEM((rows, NY, block), BF16),
                pltpu.VMEM((nz, NY, chunk), BF16),
                pltpu.VMEM((nf, 1, LANES), F32),
                pltpu.VMEM((NY, 1, LANES), F32),
                pltpu.VMEM((nz, 1, LANES), F32),
                pltpu.VMEM((nf, share_rows, LANES), F32),
                pltpu.VMEM((nf, share_rows, LANES), F32),
                pltpu.VMEM((NY, share_rows, LANES), F32),
                pltpu.VMEM((nz, share_rows, LANES), F32),
                pltpu.VMEM((nf, share_rows, LANES), F32),
                pltpu.VMEM((nf * share_rows, LANES), F32),
                pltpu.VMEM((NY, nz, parts, LANES), F32),
                pltpu.VMEM((rows * tiles, LANES), F32),
                pltpu.VMEM((rows * tiles, LANES), F32),
                pltpu.VMEM((nf, NY, rows * tiles, LANES), BF16),
                pltpu.VMEM((tiles * nf * rows, LANES), F32),
                pltpu.SemaphoreType.REGULAR,
                dma((4,)),
                dma((2, NY)),
                dma((2,)),
                dma((2,)),
                dma((2,)),
                dma((2,)),
                dma((2,)),
                dma((2,)),
                dma((2,)),
                dma((2,)),
                dma((2,)),
                dma((1,)),
                dma((nz,)),
                dma((1,)),
                dma((NY,)),
                dma((1,)),
                dma((NY,)),
                dma((1,)),
                dma((NY,)),
            ],
            compiler_params=pltpu.CompilerParams(
                collective_id=0, has_side_effects=True, vmem_limit_bytes=16 * 2**20
            ),
        )(*(pltpu.with_memory_space_constraint(value, pltpu.HBM) for value in (deltas, momentum, master)))
        return pl.pallas_call(
            functools.partial(copy_kernel, len(outs)),
            out_shape=outs,
            in_specs=[pl.BlockSpec(memory_space=pltpu.VMEM)] * len(outs),
            out_specs=(anywhere,) * len(outs),
            scratch_shapes=[dma((len(outs),))],
            compiler_params=pltpu.CompilerParams(vmem_limit_bytes=16 * 2**20),
        )(*results)

    placed = (P("rep", "fsdp", None), P("fsdp", None), P("fsdp", None))
    return jax.shard_map(
        body,
        mesh=mesh,
        in_specs=placed,
        out_specs=(P("fsdp", None), P("fsdp", None), P()),
        check_vma=False,
    )
```
